256 devices in a mesh: prompt: 8 (over x, y_hi), tile: 32 (over y_lo, z, core).
Axes of the slice: x: 4, y: 4 (y_hi: 2, y_lo: 2; y = y_hi * 2 + y_lo), z: 8, core: 2. Of those that a mesh axis runs over, the one named last changes fastest.
Arguments:
- latent: bfloat16 [1024, 160, 16], P(('prompt', 'tile')), parts along dimension 0, may hold values from -6 to 6
- cached_latent: bfloat16 [2, 1024, 160, 16], P(None, ('prompt', 'tile')), parts along dimension 1, may hold values from -6 to 6
- cached_features: bfloat16 [2, 1024, 160, 384], P(None, ('prompt', 'tile')), parts along dimension 1, may hold values from -5 to 5
- reward_grad: bfloat16 [2048, 320, 192], P(('prompt', 'tile')), parts along dimension 0, may hold values from -6 to 6
- conv_in_weight: bfloat16 [3, 3, 3, 16, 384], replicated, may hold values from -0.3125 to 0.3125
- conv_mid_weight: bfloat16 [3, 3, 3, 384, 384], replicated, may hold values from -0.0625 to 0.0625
- conv_up_weight: bfloat16 [3, 3, 384, 192], replicated, may hold values from -0.109375 to 0.109375
- norm_gain: float32 [384], replicated, may hold values from 0.5 to 1.5
- out_gain: float32 [192], replicated, may hold values from 0.5 to 1.5
- shard_order: int32 [256], P('prompt'), parts along dimension 0, may hold values from 0 to 31, each once
Outputs:
- token_grad: float32 [40960, 64], P(('prompt', 'tile')), parts along dimension 0
The draws below stay inside these ranges and needn't reach their ends.
There are 8 independent parts, one for each index of `prompt`. The reference program is written for one: setup_inputs(seed, part) draws one part's arguments, and reference() takes and returns one part's arrays. A program takes and returns all parts, laid end to end along the dimension named above; an argument that names none is the same for every part. Nothing has to cross between parts.
Inputs may be any that keep to these rules, and one draw needn't show every extreme that they name: shard_order is a permutation: each of 0 to 31 once.
All inputs are finite; a program needn't handle non-finite values.
Results may differ from the reference program's by a relative error of at most 0.0095.
Values may be sent and summed in bfloat16 or wider, within the bound.
A program may use at most 64 MiB of HBM per device.

```python
import jax
import jax.numpy as jnp
from jax import lax

LAT = 16
C_MID = 384
C_OUT = 192
COLS = 160
HEIGHT = 128
TOKENS = 5120
PIECE = 5
N_TILE = 32


def shard_levels(own_key, extent, pieces, least, largest):
    def one(dim, blocks):
        heights = jax.random.uniform(jax.random.fold_in(jax.random.fold_in(own_key, 6), dim), (blocks,), jnp.float32, least / len(pieces), largest / len(pieces))
        return jnp.repeat(jnp.exp(heights), extent[dim] // blocks).reshape((-1,) + (1,) * (len(extent) - dim - 1))

    gain = one(*pieces[0])
    for cut in pieces[1:]:
        gain = gain * one(*cut)
    return gain


def noise(rng, dims, scale, limit, cuts=(), kind=jnp.bfloat16):
    level = shard_levels(rng, dims, cuts, -0.22, 0.18) if cuts else 1.0
    drawn = jax.random.normal(rng, dims, jnp.float32) * scale * level
    return jnp.minimum(jnp.maximum(drawn, -limit), limit).astype(kind)


def setup_inputs(seed: int = 0, part: int = 0) -> dict:
    key_of = jax.random.split(jax.random.key(seed), 11)
    part_splits = jax.random.split(jax.random.fold_in(key_of[10], part), 11)
    latent = noise(part_splits[0], (HEIGHT, COLS, LAT), 1.0, 6.0, ((0, 32),))
    cached_latent = noise(part_splits[1], (2, HEIGHT, COLS, LAT), 1.0, 6.0, ((1, 32),))
    cached_features = noise(part_splits[2], (2, HEIGHT, COLS, C_MID), 0.8, 5.0, ((1, 32),))
    reward_grad = noise(part_splits[3], (2 * HEIGHT, 2 * COLS, C_OUT), 1.0, 6.0, ((0, 32),))
    conv_in_weight = noise(key_of[4], (3, 3, 3, LAT, C_MID), (27 * LAT) ** -0.5, 0.3125)
    conv_mid_weight = noise(key_of[5], (3, 3, 3, C_MID, C_MID), (27 * C_MID) ** -0.5, 0.0625)
    conv_up_weight = noise(key_of[6], (3, 3, C_MID, C_OUT), (9 * C_MID) ** -0.5, 0.109375)
    norm_gain = jnp.clip(jax.random.uniform(key_of[7], (C_MID,), jnp.float32, 0.5, 1.5), 0.5, 1.5)
    out_gain = jnp.clip(jax.random.uniform(key_of[8], (C_OUT,), jnp.float32, 0.5, 1.5), 0.5, 1.5)
    shard_order = jax.random.permutation(part_splits[9], N_TILE).astype(jnp.int32)
    return dict(latent=latent, cached_latent=cached_latent, cached_features=cached_features, reward_grad=reward_grad, conv_in_weight=conv_in_weight, conv_mid_weight=conv_mid_weight, conv_up_weight=conv_up_weight, norm_gain=norm_gain, out_gain=out_gain, shard_order=shard_order)


epsilon = 1e-06
highest = lax.Precision.HIGHEST

def norm_silu(values, gain_vector):
    scaled = values * lax.rsqrt(lax.optimization_barrier(jnp.mean(values * values, axis=-1, keepdims=True)) + epsilon)
    return jax.nn.silu(scaled * gain_vector)

def causal_conv(frames, kernel):
    result = lax.conv_general_dilated(frames.astype(jnp.float32)[None], kernel.astype(jnp.float32), (1, 1, 1), ((0, 0), (1, 1), (1, 1)), dimension_numbers=('NDHWC', 'DHWIO', 'NDHWC'), precision=highest)
    return result[0, 0]

def plane_conv(plane_in, kernel):
    result = lax.conv_general_dilated(plane_in.astype(jnp.float32)[None], kernel.astype(jnp.float32), (1, 1), ((1, 1), (1, 1)), dimension_numbers=('NHWC', 'HWIO', 'NHWC'), precision=highest)
    return result[0]

def plane_back(grad_in, kernel):
    flipped = kernel[::-1, ::-1].astype(jnp.float32)
    result = lax.conv_general_dilated(grad_in.astype(jnp.float32)[None], flipped, (1, 1), ((1, 1), (1, 1)), dimension_numbers=('NHWC', 'HWOI', 'NHWC'), precision=highest)
    return result[0]

def reference(latent, cached_latent, cached_features, reward_grad, conv_in_weight, conv_mid_weight, conv_up_weight, norm_gain, out_gain, shard_order):
    latent_frames = jnp.concatenate([cached_latent, latent[None]], axis=0)
    hidden = lax.optimization_barrier(causal_conv(latent_frames, conv_in_weight).astype(jnp.bfloat16))
    hidden_wide = hidden.astype(jnp.float32)
    activated = norm_silu(hidden_wide, norm_gain).astype(jnp.bfloat16)
    feature_frames = jnp.concatenate([cached_features, activated[None]], axis=0)
    block_state = (hidden_wide + causal_conv(feature_frames, conv_mid_weight)).astype(jnp.bfloat16)
    doubled = jnp.repeat(jnp.repeat(block_state, 2, axis=0), 2, axis=1)
    upper_plane = lax.optimization_barrier(plane_conv(doubled, conv_up_weight).astype(jnp.bfloat16))
    upper_wide = upper_plane.astype(jnp.float32)
    outcome, pullback = jax.vjp(lambda values: norm_silu(values, out_gain), upper_wide)
    upper_grad = pullback(reward_grad.astype(jnp.float32))[0].astype(jnp.bfloat16)
    doubled_grad = plane_back(upper_grad, conv_up_weight)
    block_grad = lax.optimization_barrier(doubled_grad.reshape(HEIGHT, 2, COLS, 2, C_MID).sum(axis=(1, 3)).astype(jnp.bfloat16))
    activated_grad = plane_back(block_grad, conv_mid_weight[2])
    ignored, hidden_pull = jax.vjp(lambda values: norm_silu(values, norm_gain), hidden_wide)
    hidden_grad = (block_grad.astype(jnp.float32) + hidden_pull(activated_grad)[0]).astype(jnp.bfloat16)
    latent_grad = plane_back(hidden_grad, conv_in_weight[2])
    patches = latent_grad.reshape(HEIGHT // 2, 2, COLS // 2, 2, LAT).transpose(0, 2, 1, 3, 4)
    patches = patches.reshape(N_TILE, N_TILE, PIECE, 4 * LAT)
    swapped = jnp.transpose(patches, (1, 0, 2, 3))
    placed = jnp.zeros_like(swapped).at[:, shard_order].set(swapped)
    return placed.reshape(TOKENS, 4 * LAT)
```

```python
import jax
import jax.numpy as jnp
from jax import lax
from jax.experimental import pallas as pl
from jax.experimental.pallas import tpu as pltpu
from jax.sharding import PartitionSpec as P

EPS = 1e-06
F32 = jnp.float32
BF16 = jnp.bfloat16
ROWS = 4
COLS = 160
LAT = 16
MID = 384
OUT = 192
TILES = 32
PIECE = 5
TOK = 80


def iota(shape, dim):
    return lax.broadcasted_iota(jnp.int32, shape, dim)


def down(x):
    return jnp.where(iota(x.shape, 0) == 0, 0.0, pltpu.roll(x, 1, 0))


def up(x):
    n = x.shape[0]
    return jnp.where(iota(x.shape, 0) == n - 1, 0.0, pltpu.roll(x, n - 1, 0))


def mixed(x, low, high):
    a, b, c = x[:, :128], x[:, 128:256], x[:, 256:]
    middle = jnp.where(iota(b.shape, 1) < 64, low(b), high(b))
    return jnp.concatenate([low(a), middle, high(c)], axis=1)


def halves_mean(x):
    a, b, c = x[:, :128], x[:, 128:256], x[:, 256:]
    left = iota(b.shape, 1) < 64
    first = jnp.sum(a + jnp.where(left, b, 0.0), axis=1, keepdims=True) * (1.0 / OUT)
    second = jnp.sum(c + jnp.where(left, 0.0, b), axis=1, keepdims=True) * (1.0 / OUT)
    return first, second


def spread(first, second, rows):
    left = iota((rows, 128), 1) < 64
    one = jnp.broadcast_to(first, (rows, 128))
    two = jnp.broadcast_to(second, (rows, 128))
    return jnp.concatenate([one, jnp.where(left, one, two), two], axis=1)


def sigmoid(x):
    return 0.5 + 0.5 * jnp.tanh(0.5 * x)


def cotangent(normed, gain, grad):
    u = normed * gain
    s = sigmoid(u)
    return grad * gain * (s * (1.0 + u * (1.0 - s)))


def dot(a, b):
    return jnp.dot(a, b, preferred_element_type=F32)


def dot_t(a, b):
    return lax.dot_general(a, b, (((1,), (1,)), ((), ())), preferred_element_type=F32)


def kernel(
    lat_in, latc_in, feat_in, rew_in, win_in, wmid_in, wup_in, gain_ref, ogain_ref, order_ref,
    out_ref,
    lat, feat, hid, xs, rew, rewf, rewp, win, wmid, wback, wup, fold, vt,
    psend, precv, bg, zs, tsend, trecv, place,
    local_sem, halo_send, halo_recv, x_send, x_recv, p_send, p_recv, b_send, b_recv,
    t_send, t_recv, know_sem,
):
    me = lax.axis_index("tile")

    def at(offset):
        return {"tile": lax.rem(me + (offset + TILES), TILES)}

    def signal(sem, offset):
        pl.semaphore_signal(sem, inc=1, device_id=at(offset), device_id_type=pl.DeviceIdType.MESH)

    def remote(src, dst, send, recv, offset):
        return pltpu.make_async_remote_copy(
            src_ref=src, dst_ref=dst, send_sem=send, recv_sem=recv,
            device_id=at(offset), device_id_type=pl.DeviceIdType.MESH,
        )

    local = []

    def load(src, dst):
        copy = pltpu.make_async_copy(src, dst, local_sem.at[len(local)])
        copy.start()
        local.append(copy)
        return copy

    barrier = pltpu.get_barrier_semaphore()
    signal(barrier, -1)
    signal(barrier, 1)
    load_lat = [
        load(lat_in, lat.at[2, pl.ds(2, ROWS)]),
        load(latc_in, lat.at[pl.ds(0, 2), pl.ds(2, ROWS)]),
    ]
    load_win = load(win_in, win)
    load_wup = load(wup_in, wup)
    load_rew = load(rew_in, rew)
    load_feat = load(feat_in, feat.at[pl.ds(0, 2), pl.ds(1, ROWS)])
    load_mid = []
    for t in (0, 1, 2):
        for j in range(3):
            load_mid.append(load(wmid_in.at[t, :, j], wmid.at[t, :, :, pl.ds(j * MID, MID)]))
    load_back = []
    for i in range(3):
        load_back.append(load(wmid_in.at[2, i], wback.at[:, :, pl.ds(i * MID, MID)]))

    pl.semaphore_wait(barrier, 2)
    halo = []
    for side, offset in ((0, -1), (1, 1)):
        row = 0 if side == 0 else ROWS - 2
        land = ROWS + 2 if side == 0 else 0
        copies = [
            remote(lat_in.at[pl.ds(row, 2)], lat.at[2, pl.ds(land, 2)],
                   halo_send.at[side, 0], halo_recv.at[side, 0], offset),
            remote(latc_in.at[:, pl.ds(row, 2)], lat.at[pl.ds(0, 2), pl.ds(land, 2)],
                   halo_send.at[side, 1], halo_recv.at[side, 1], offset),
        ]
        row = 0 if side == 0 else ROWS - 1
        land = ROWS + 1 if side == 0 else 0
        copies.append(
            remote(feat_in.at[:, pl.ds(row, 1)], feat.at[pl.ds(0, 2), pl.ds(land, 1)],
                   halo_send.at[side, 2], halo_recv.at[side, 2], offset))
        halo.append(copies)
    for n in range(3):
        for side in range(2):
            halo[side][n].start()
    signal(know_sem.at[0], -1)
    signal(know_sem.at[0], 1)

    load_wup.wait()
    parts = []
    for i in range(3):
        k0, k1, k2 = (wup[i, j].astype(F32) for j in range(3))
        parts.append(jnp.concatenate(
            [jnp.concatenate([k0, k2], axis=1), jnp.concatenate([k1 + k2, k0 + k1], axis=1)],
            axis=1))
    fold[0, :MID] = parts[0].astype(BF16)
    fold[0, MID:] = (parts[1] + parts[2]).astype(BF16)
    fold[1, :MID] = (parts[0] + parts[1]).astype(BF16)
    fold[1, MID:] = parts[2].astype(BF16)

    load_rew.wait()
    rewf[1] = jnp.zeros((2 * COLS, 128), F32)
    for y in range(2 * ROWS):
        rewf[0] = rew[y, :, :128].astype(F32)
        rewf[1, :, :OUT - 128] = rew[y, :, 128:].astype(F32)
        e0, e1 = (rewf[n, pl.ds(0, COLS, stride=2), :] for n in range(2))
        o0, o1 = (pltpu.roll(rewf[n, pl.ds(1, COLS, stride=2), :], 64, 1) for n in range(2))
        left = iota((COLS, 128), 1) < 64
        rewp[y] = jnp.concatenate(
            [e0, jnp.where(left, e1, o0), jnp.where(left, o0, o1)], axis=1).astype(BF16)

    load_win.wait()
    r = iota((1024, 144), 0)
    par = lax.shift_right_logical(r, 9)
    d = lax.shift_right_logical(r, 7) & 3
    d = jnp.where(d == 3, -1, d)
    extra = lax.shift_right_logical(r, 6) & 1
    a = lax.shift_right_logical(r, 5) & 1
    b = lax.shift_right_logical(r, 4) & 1
    c = r & 15
    i = jnp.where(extra == 0, jnp.where(par == 0, a + 1, a), jnp.where(par == 0, 0, 2))
    fits = jnp.where(extra == 0, 1, jnp.where(par == 0, a, 1 - a))
    j = b - d + 1
    fits = jnp.where((j >= 0) & (j <= 2), fits, 0)
    want = jnp.where(fits == 1, i * 48 + j * 16 + c, -1)
    pick = jnp.where(iota((1024, 144), 1) == want, 1.0, 0.0).astype(BF16)
    vt[...] = dot(pick, win[2].reshape(144, MID)).astype(BF16)
    zs[:, :, 0:8] = jnp.zeros((ROWS, 4, 8, 128), F32)
    zs[:, :, COLS + 8:] = jnp.zeros((ROWS, 4, 8, 128), F32)

    lane = lax.shift_right_logical(iota((1, 256), 1), 3)
    own_at = jnp.full((1, 256), -1, jnp.int32)
    edge_at = jnp.full((1, 256), -1, jnp.int32)
    for t in range(TILES):
        own_at = jnp.where(lane == t, order_ref[t], own_at)
        after = order_ref[t + 1] if t + 1 < TILES else jnp.int32(-1)
        before = order_ref[t - 1] if t > 0 else jnp.int32(-1)
        edge_at = jnp.where(lane == t, jnp.where(me < TILES // 2, after, before), edge_at)
    row = iota((TILES * PIECE, 256), 0)
    block = lax.shift_right_logical(row * 205, 10)
    same = (row - block * PIECE) == (iota((TILES * PIECE, 256), 1) & 7)
    place[0] = jnp.where(same & (block == own_at), 1.0, 0.0).astype(BF16)
    place[1] = jnp.where(same & (block == edge_at), 1.0, 0.0).astype(BF16)

    for copy in load_lat:
        copy.wait()
    for n in range(2):
        for side in range(2):
            halo[side][n].wait_recv()

    @pl.when(me == 0)
    def _():
        lat[:, 0:2] = jnp.zeros((3, 2, COLS, LAT), BF16)

    @pl.when(me == TILES - 1)
    def _():
        lat[:, ROWS + 2:] = jnp.zeros((3, 2, COLS, LAT), BF16)

    taps = []
    for h in range(ROWS + 4):
        x = jnp.concatenate([lat[t, h].astype(F32) for t in range(3)], axis=1)
        taps.append(jnp.concatenate([down(x), x, up(x)], axis=1).astype(BF16))
    total = None
    for i in range(3):
        weight = jnp.concatenate([win[t, i, j] for j in range(3) for t in range(3)], axis=0)
        part = dot(jnp.concatenate(taps[i:i + ROWS + 2], axis=0), weight)
        total = part if total is None else total + part
    gain = gain_ref[...]
    for h in range(ROWS + 2):
        value = total[h * COLS:(h + 1) * COLS].astype(BF16)
        hid[h] = value
        v = value.astype(F32)
        u = v * lax.rsqrt(jnp.mean(v * v, axis=1, keepdims=True) + EPS) * gain
        feat[2, h] = (u * sigmoid(u)).astype(BF16)

    load_feat.wait()
    for side in range(2):
        halo[side][2].wait_recv()

    @pl.when(me == 0)
    def _():
        feat[:, 0] = jnp.zeros((3, COLS, MID), BF16)

    @pl.when(me == TILES - 1)
    def _():
        feat[:, ROWS + 1] = jnp.zeros((3, COLS, MID), BF16)

    for copy in load_mid:
        copy.wait()
    pl.semaphore_wait(know_sem.at[0], 2)
    signal(know_sem.at[1], -2)
    signal(know_sem.at[1], 2)

    def middle(rows):
        left = jnp.concatenate(
            [jnp.concatenate([feat[t, h + i] for t in range(3) for i in range(3)], axis=1)
             for h in rows], axis=0)
        y = dot(left, wmid[...].reshape(9 * MID, 3 * MID))
        for n, h in enumerate(rows):
            z = y[n * COLS:(n + 1) * COLS]
            value = z[:, MID:2 * MID] + down(z[:, :MID]) + up(z[:, 2 * MID:])
            xs[h + 1] = (hid[h + 1].astype(F32) + value).astype(BF16)

    middle((0, 3))
    x_up = remote(xs.at[1], xs.at[ROWS + 1], x_send.at[0], x_recv.at[0], -1)
    x_down = remote(xs.at[ROWS], xs.at[0], x_send.at[1], x_recv.at[1], 1)
    x_up.start()
    x_down.start()
    pl.semaphore_wait(know_sem.at[1], 2)
    signal(know_sem.at[2], -4)
    signal(know_sem.at[2], 4)
    middle((1, 2))
    pl.semaphore_wait(know_sem.at[2], 2)
    signal(know_sem.at[3], -8)
    signal(know_sem.at[3], 8)
    x_up.wait_recv()
    x_down.wait_recv()

    @pl.when(me == 0)
    def _():
        xs[0] = jnp.zeros((COLS, MID), BF16)

    @pl.when(me == TILES - 1)
    def _():
        xs[ROWS + 1] = jnp.zeros((COLS, MID), BF16)

    ogain = ogain_ref[...]

    def upper(a, rows):
        left = jnp.concatenate(
            [jnp.concatenate([xs[h + a], xs[h + a + 1]], axis=1) for h in rows], axis=0)
        y = dot(left, fold[a])
        lefts = []
        for n, h in enumerate(rows):
            z = y[n * COLS:(n + 1) * COLS]
            v = (z[:, MID:] + mixed(z[:, :MID], down, up)).astype(BF16).astype(F32)
            one, two = halves_mean(v * v)
            scale = spread(lax.rsqrt(one + EPS), lax.rsqrt(two + EPS), COLS)
            normed = v * scale
            t = cotangent(normed, ogain, rewp[2 * h + a].astype(F32))
            one, two = halves_mean(t * normed)
            g = (scale * (t - normed * spread(one, two, COLS))).astype(BF16)
            lefts.append(jnp.concatenate([mixed(g.astype(F32), up, down).astype(BF16), g], axis=1))
        z = dot_t(jnp.concatenate(lefts, axis=0), fold[a])
        return {h: (z[n * COLS:(n + 1) * COLS, :MID], z[n * COLS:(n + 1) * COLS, MID:])
                for n, h in enumerate(rows)}

    z0 = upper(0, (0, 1))
    psend[0] = z0[0][0].astype(BF16)
    p_up = remote(psend.at[0], precv.at[1], p_send.at[0], p_recv.at[0], -1)
    p_up.start()
    z1 = upper(1, (2, 3))
    psend[1] = z1[3][1].astype(BF16)
    p_down = remote(psend.at[1], precv.at[0], p_send.at[1], p_recv.at[1], 1)
    p_down.start()
    z0.update(upper(0, (2, 3)))
    z1.update(upper(1, (0, 1)))
    p_up.wait_recv()
    p_down.wait_recv()

    @pl.when(me == 0)
    def _():
        precv[0] = jnp.zeros((COLS, MID), BF16)

    @pl.when(me == TILES - 1)
    def _():
        precv[1] = jnp.zeros((COLS, MID), BF16)

    bg[1] = (z0[0][1] + z0[1][0] + z1[0][0] + precv[0].astype(F32)).astype(BF16)
    bg[ROWS] = (z0[3][1] + precv[1].astype(F32) + z1[3][0] + z1[2][1]).astype(BF16)
    b_up = remote(bg.at[1], bg.at[ROWS + 1], b_send.at[0], b_recv.at[0], -1)
    b_down = remote(bg.at[ROWS], bg.at[0], b_send.at[1], b_recv.at[1], 1)
    b_up.start()
    b_down.start()
    for h in (1, 2):
        bg[h + 1] = (z0[h][1] + z0[h + 1][0] + z1[h][0] + z1[h - 1][1]).astype(BF16)

    for copy in load_back:
        copy.wait()

    def lower(rows):
        left = jnp.concatenate(
            [jnp.concatenate([bg[h + 2], bg[h + 1], bg[h]], axis=1) for h in rows], axis=0)
        y = dot_t(left, wback[...].reshape(3 * MID, 3 * MID))
        for n, h in enumerate(rows):
            z = y[n * COLS:(n + 1) * COLS]
            grad = z[:, MID:2 * MID] + up(z[:, :MID]) + down(z[:, 2 * MID:])
            v = hid[h + 1].astype(F32)
            scale = lax.rsqrt(jnp.mean(v * v, axis=1, keepdims=True) + EPS)
            normed = v * scale
            t = cotangent(normed, gain, grad)
            m = jnp.mean(t * normed, axis=1, keepdims=True)
            g = (bg[h + 1].astype(F32) + scale * (t - normed * m)).astype(BF16)
            last = dot_t(g, vt[(h % 2) * 512:(h % 2) * 512 + 512])
            for p in range(4):
                zs[h, p, 8:COLS + 8] = last[:, p * 128:(p + 1) * 128]

    lower((1, 2))
    b_up.wait_recv()
    b_down.wait_recv()

    @pl.when(me == 0)
    def _():
        bg[0] = jnp.zeros((COLS, MID), BF16)

    @pl.when(me == TILES - 1)
    def _():
        bg[ROWS + 1] = jnp.zeros((COLS, MID), BF16)

    lower((0, 3))

    def tokens(h):
        picks = ((0, 0), (1, 1), (2, 2), (3, -1))
        parts = [zs[h, n, pl.ds(8 + d, TOK, stride=2), :] for n, d in picks]
        return (parts[0] + parts[1]) + (parts[2] + parts[3])

    u0, u1, u2, u3 = (tokens(h) for h in range(ROWS))
    low = iota((TOK, 128), 1) < 64
    m0 = jnp.where(low, u0 + u1 + pltpu.roll(u2, 64, 1), u3)
    m1 = jnp.where(low, u2 + u3 + pltpu.roll(u1, 64, 1), u0)
    both = jnp.concatenate([m0, m1], axis=0).astype(BF16)
    row = iota((256, TILES * PIECE), 0)
    source = lax.shift_right_logical(row, 3) * PIECE + (row & 7)
    take = ((row & 7) < PIECE) & (iota((256, TILES * PIECE), 1) == source)
    blocks = dot(jnp.where(take, 1.0, 0.0).astype(BF16), both)
    tsend[...] = blocks.reshape(TILES, 8, 128).astype(BF16)

    pl.semaphore_wait(know_sem.at[3], 2)

    def block_copy(k):
        to = lax.rem(me + k, TILES)
        return pltpu.make_async_remote_copy(
            src_ref=tsend.at[to], dst_ref=trecv.at[me], send_sem=t_send.at[k],
            recv_sem=t_recv.at[k],
            device_id={"tile": to}, device_id_type=pl.DeviceIdType.MESH)

    for k in range(1, TILES):
        block_copy(k).start()
    trecv[me] = tsend[me]
    for k in range(1, TILES):
        source = lax.rem(me + (TILES - k), TILES)
        pltpu.make_async_remote_copy(
            src_ref=tsend.at[source], dst_ref=trecv.at[source], send_sem=t_send.at[k],
            recv_sem=t_recv.at[k],
            device_id={"tile": source}, device_id_type=pl.DeviceIdType.MESH).wait_recv()
    got = trecv[...].astype(F32).reshape(TILES * 8, 128).astype(BF16)
    own = dot(place[0], got)
    edge = dot(place[1], got)
    out_ref[...] = (own + pltpu.roll(edge, 64, 1))[:, :64]

    for copies in halo:
        for copy in copies:
            copy.wait_send()
    for copy in (x_up, x_down, p_up, p_down, b_up, b_down):
        copy.wait_send()
    for k in range(1, TILES):
        block_copy(k).wait_send()


def shards(latent, cached_latent, cached_features, reward_grad, conv_in_weight, conv_mid_weight,
           conv_up_weight, norm_gain, out_gain, shard_order):
    hbm = pl.BlockSpec(memory_space=pltpu.HBM)
    vmem = pl.BlockSpec(memory_space=pltpu.VMEM)
    smem = pl.BlockSpec(memory_space=pltpu.SMEM)
    dma = pltpu.SemaphoreType.DMA
    call = pl.pallas_call(
        kernel,
        out_shape=jax.ShapeDtypeStruct((TILES * PIECE, 4 * LAT), F32),
        in_specs=[hbm] * 7 + [vmem, vmem, smem],
        out_specs=vmem,
        scratch_shapes=[
            pltpu.VMEM((3, ROWS + 4, COLS, LAT), BF16),
            pltpu.VMEM((3, ROWS + 2, COLS, MID), BF16),
            pltpu.VMEM((ROWS + 2, COLS, MID), BF16),
            pltpu.VMEM((ROWS + 2, COLS, MID), BF16),
            pltpu.VMEM((2 * ROWS, 2 * COLS, OUT), BF16),
            pltpu.VMEM((2, 2 * COLS, 128), F32),
            pltpu.VMEM((2 * ROWS, COLS, 2 * OUT), BF16),
            pltpu.VMEM((3, 3, 3, LAT, MID), BF16),
            pltpu.VMEM((3, 3, MID, 3 * MID), BF16),
            pltpu.VMEM((3, MID, 3 * MID), BF16),
            pltpu.VMEM((3, 3, MID, OUT), BF16),
            pltpu.VMEM((2, 2 * MID, 4 * OUT), BF16),
            pltpu.VMEM((1024, MID), BF16),
            pltpu.VMEM((2, COLS, MID), BF16),
            pltpu.VMEM((2, COLS, MID), BF16),
            pltpu.VMEM((ROWS + 2, COLS, MID), BF16),
            pltpu.VMEM((ROWS, 4, COLS + 16, 128), F32),
            pltpu.VMEM((TILES, 8, 128), BF16),
            pltpu.VMEM((TILES, 8, 128), BF16),
            pltpu.VMEM((2, TILES * PIECE, 256), BF16),
            dma((18,)), dma((2, 3)), dma((2, 3)), dma((2,)), dma((2,)), dma((2,)), dma((2,)),
            dma((2,)), dma((2,)), dma((TILES,)), dma((TILES,)),
            pltpu.SemaphoreType.REGULAR((4,)),
        ],
        compiler_params=pltpu.CompilerParams(
            collective_id=0, has_side_effects=True, vmem_limit_bytes=60 << 20),
    )
    return call(latent, cached_latent, cached_features, reward_grad, conv_in_weight,
                conv_mid_weight, conv_up_weight, norm_gain[None, :],
                jnp.concatenate([out_gain, out_gain])[None, :], shard_order)


def solution(mesh):
    part = P(("prompt", "tile"), None, None)
    frames = P(None, ("prompt", "tile"), None, None)
    return jax.shard_map(
        shards,
        mesh=mesh,
        in_specs=(part, frames, frames, part, P(), P(), P(), P(), P(), P("prompt")),
        out_specs=P(("prompt", "tile"), None),
        check_vma=False,
    )
```

```python
import jax
import jax.numpy as jnp
from jax import lax
from jax.experimental import pallas as pl
from jax.experimental.pallas import tpu as pltpu
from jax.sharding import PartitionSpec as P

EPS = 1e-06
F32 = jnp.float32
BF16 = jnp.bfloat16
ROWS = 4
COLS = 160
LAT = 16
MID = 384
OUT = 192
TILES = 32
PIECE = 5
TOK = 80


def iota(shape, dim):
    return lax.broadcasted_iota(jnp.int32, shape, dim)


def down(x):
    return jnp.where(iota(x.shape, 0) == 0, 0.0, pltpu.roll(x, 1, 0))


def up(x):
    n = x.shape[0]
    return jnp.where(iota(x.shape, 0) == n - 1, 0.0, pltpu.roll(x, n - 1, 0))


def mixed(x, low, high):
    a, b, c = x[:, :128], x[:, 128:256], x[:, 256:]
    middle = jnp.where(iota(b.shape, 1) < 64, low(b), high(b))
    return jnp.concatenate([low(a), middle, high(c)], axis=1)


def halves_mean(x):
    a, b, c = x[:, :128], x[:, 128:256], x[:, 256:]
    left = iota(b.shape, 1) < 64
    first = jnp.sum(a + jnp.where(left, b, 0.0), axis=1, keepdims=True) * (1.0 / OUT)
    second = jnp.sum(c + jnp.where(left, 0.0, b), axis=1, keepdims=True) * (1.0 / OUT)
    return first, second


def spread(first, second, rows):
    left = iota((rows, 128), 1) < 64
    one = jnp.broadcast_to(first, (rows, 128))
    two = jnp.broadcast_to(second, (rows, 128))
    return jnp.concatenate([one, jnp.where(left, one, two), two], axis=1)


def sigmoid(x):
    return 0.5 + 0.5 * jnp.tanh(0.5 * x)


def cotangent(normed, gain, grad):
    u = normed * gain
    s = sigmoid(u)
    return grad * gain * (s * (1.0 + u * (1.0 - s)))


def dot(a, b):
    return jnp.dot(a, b, preferred_element_type=F32)


def dot_t(a, b):
    return lax.dot_general(a, b, (((1,), (1,)), ((), ())), preferred_element_type=F32)


def kernel(
    lat_in, latc_in, feat_in, rew_in, win_in, wmid_in, wup_in, gain_ref, ogain_ref, order_ref,
    out_ref,
    lat, feat, hid, xs, rew, rewp, win, wmid, wback, wup, fold, vt,
    psend, precv, bg, zs, tsend, trecv, place,
    local_sem, halo_send, halo_recv, x_send, x_recv, p_send, p_recv, b_send, b_recv,
    t_send, t_recv, know_sem,
):
    me = lax.axis_index("tile")

    def at(offset):
        return {"tile": lax.rem(me + (offset + TILES), TILES)}

    def signal(sem, offset):
        pl.semaphore_signal(sem, inc=1, device_id=at(offset), device_id_type=pl.DeviceIdType.MESH)

    def remote(src, dst, send, recv, offset):
        return pltpu.make_async_remote_copy(
            src_ref=src, dst_ref=dst, send_sem=send, recv_sem=recv,
            device_id=at(offset), device_id_type=pl.DeviceIdType.MESH,
        )

    local = []

    def load(src, dst):
        copy = pltpu.make_async_copy(src, dst, local_sem.at[len(local)])
        copy.start()
        local.append(copy)
        return copy

    barrier = pltpu.get_barrier_semaphore()
    signal(barrier, -1)
    signal(barrier, 1)
    load_lat = [
        load(lat_in, lat.at[2, pl.ds(2, ROWS)]),
        load(latc_in, lat.at[pl.ds(0, 2), pl.ds(2, ROWS)]),
    ]
    load_win = load(win_in, win)
    load_wup = load(wup_in, wup)
    load_rew = load(rew_in, rew)
    load_feat = load(feat_in, feat.at[pl.ds(0, 2), pl.ds(1, ROWS)])
    load_mid = []
    for t in (0, 1, 2):
        for j in range(3):
            load_mid.append(load(wmid_in.at[t, :, j], wmid.at[t, :, :, pl.ds(j * MID, MID)]))
    load_back = []
    for i in range(3):
        load_back.append(load(wmid_in.at[2, i], wback.at[:, :, pl.ds(i * MID, MID)]))

    pl.semaphore_wait(barrier, 2)
    halo = []
    for side, offset in ((0, -1), (1, 1)):
        row = 0 if side == 0 else ROWS - 2
        land = ROWS + 2 if side == 0 else 0
        copies = [
            remote(lat_in.at[pl.ds(row, 2)], lat.at[2, pl.ds(land, 2)],
                   halo_send.at[side, 0], halo_recv.at[side, 0], offset),
            remote(latc_in.at[:, pl.ds(row, 2)], lat.at[pl.ds(0, 2), pl.ds(land, 2)],
                   halo_send.at[side, 1], halo_recv.at[side, 1], offset),
        ]
        row = 0 if side == 0 else ROWS - 1
        land = ROWS + 1 if side == 0 else 0
        copies.append(
            remote(feat_in.at[:, pl.ds(row, 1)], feat.at[pl.ds(0, 2), pl.ds(land, 1)],
                   halo_send.at[side, 2], halo_recv.at[side, 2], offset))
        halo.append(copies)
    for n in range(3):
        for side in range(2):
            halo[side][n].start()
    signal(know_sem.at[0], -1)
    signal(know_sem.at[0], 1)

    load_wup.wait()
    parts = []
    for i in range(3):
        k0, k1, k2 = (wup[i, j].astype(F32) for j in range(3))
        parts.append(jnp.concatenate([k0, k2, k1 + k2, k0 + k1], axis=0))
    fold[0, :, :MID] = parts[0].astype(BF16)
    fold[0, :, MID:] = (parts[1] + parts[2]).astype(BF16)
    fold[1, :, :MID] = (parts[0] + parts[1]).astype(BF16)
    fold[1, :, MID:] = parts[2].astype(BF16)

    load_rew.wait()
    n = iota((2 * COLS, 2 * COLS), 0)
    column = jnp.where(n < COLS, 2 * n, 2 * n - (2 * COLS - 1))
    parting = jnp.where(iota((2 * COLS, 2 * COLS), 1) == column, 1.0, 0.0).astype(BF16)
    left = iota((COLS, 128), 1) < 64
    for y in range(2 * ROWS):
        flat = jnp.concatenate([rew[y], jnp.zeros((256 - OUT, 2 * COLS), BF16)], axis=0)
        parted = dot_t(parting, flat)
        even, odd = parted[:COLS], parted[COLS:]
        o0, o1 = pltpu.roll(odd[:, :128], 64, 1), pltpu.roll(odd[:, 128:], 64, 1)
        rewp[y] = jnp.concatenate(
            [even[:, :128], jnp.where(left, even[:, 128:], o0), jnp.where(left, o0, o1)],
            axis=1).astype(BF16)

    load_win.wait()
    r = iota((1024, 144), 0)
    par = lax.shift_right_logical(r, 9)
    d = lax.shift_right_logical(r, 7) & 3
    d = jnp.where(d == 3, -1, d)
    extra = lax.shift_right_logical(r, 6) & 1
    a = lax.shift_right_logical(r, 5) & 1
    b = lax.shift_right_logical(r, 4) & 1
    c = r & 15
    i = jnp.where(extra == 0, jnp.where(par == 0, a + 1, a), jnp.where(par == 0, 0, 2))
    fits = jnp.where(extra == 0, 1, jnp.where(par == 0, a, 1 - a))
    j = b - d + 1
    fits = jnp.where((j >= 0) & (j <= 2), fits, 0)
    want = jnp.where(fits == 1, i * 48 + j * 16 + c, -1)
    pick = jnp.where(iota((1024, 144), 1) == want, 1.0, 0.0).astype(BF16)
    vt[...] = dot(pick, win[2].reshape(144, MID)).astype(BF16)
    zs[:, :, 0:8] = jnp.zeros((ROWS, 4, 8, 128), F32)
    zs[:, :, COLS + 8:] = jnp.zeros((ROWS, 4, 8, 128), F32)

    slot = lax.shift_right_logical(iota((256, 1), 0), 3)
    own_at = jnp.full((256, 1), -1, jnp.int32)
    edge_at = jnp.full((256, 1), -1, jnp.int32)
    for t in range(TILES):
        own_at = jnp.where(slot == t, order_ref[t], own_at)
        after = order_ref[t + 1] if t + 1 < TILES else jnp.int32(-1)
        before = order_ref[t - 1] if t > 0 else jnp.int32(-1)
        edge_at = jnp.where(slot == t, jnp.where(me < TILES // 2, after, before), edge_at)
    spot = iota((256, TILES * PIECE), 1)
    block = lax.shift_right_logical(spot * 205, 10)
    same = (spot - block * PIECE) == (iota((256, TILES * PIECE), 0) & 7)
    place[0] = jnp.where(same & (block == own_at), 1.0, 0.0).astype(BF16)
    place[1] = jnp.where(same & (block == edge_at), 1.0, 0.0).astype(BF16)

    for copy in load_lat:
        copy.wait()
    for n in range(2):
        for side in range(2):
            halo[side][n].wait_recv()

    @pl.when(me == 0)
    def _():
        lat[:, 0:2] = jnp.zeros((3, 2, LAT, COLS), BF16)

    @pl.when(me == TILES - 1)
    def _():
        lat[:, ROWS + 2:] = jnp.zeros((3, 2, LAT, COLS), BF16)

    taps = []
    for h in range(ROWS + 4):
        x = jnp.concatenate([lat[t, h].astype(F32) for t in range(3)], axis=0).T
        taps.append(jnp.concatenate([down(x), x, up(x)], axis=1).astype(BF16))
    total = None
    for i in range(3):
        weight = jnp.concatenate([win[t, i, j] for j in range(3) for t in range(3)], axis=0)
        part = dot(jnp.concatenate(taps[i:i + ROWS + 2], axis=0), weight)
        total = part if total is None else total + part
    gain = gain_ref[...].reshape(1, MID)
    for h in range(ROWS + 2):
        value = total[h * COLS:(h + 1) * COLS].astype(BF16)
        hid[h] = value
        v = value.astype(F32)
        u = v * lax.rsqrt(jnp.mean(v * v, axis=1, keepdims=True) + EPS) * gain
        feat[2, h] = (u * sigmoid(u)).astype(BF16)

    load_feat.wait()
    for side in range(2):
        halo[side][2].wait_recv()

    @pl.when(me == 0)
    def _():
        feat[:, 0] = jnp.zeros((3, COLS, MID), BF16)

    @pl.when(me == TILES - 1)
    def _():
        feat[:, ROWS + 1] = jnp.zeros((3, COLS, MID), BF16)

    for copy in load_mid:
        copy.wait()
    pl.semaphore_wait(know_sem.at[0], 2)
    signal(know_sem.at[1], -2)
    signal(know_sem.at[1], 2)

    def middle(rows):
        left = jnp.concatenate(
            [jnp.concatenate([feat[t, h + i] for t in range(3) for i in range(3)], axis=1)
             for h in rows], axis=0)
        y = dot(left, wmid[...].reshape(9 * MID, 3 * MID))
        for n, h in enumerate(rows):
            z = y[n * COLS:(n + 1) * COLS]
            value = z[:, MID:2 * MID] + down(z[:, :MID]) + up(z[:, 2 * MID:])
            xs[h + 1] = (hid[h + 1].astype(F32) + value).astype(BF16)

    middle((0, 3))
    x_up = remote(xs.at[1], xs.at[ROWS + 1], x_send.at[0], x_recv.at[0], -1)
    x_down = remote(xs.at[ROWS], xs.at[0], x_send.at[1], x_recv.at[1], 1)
    x_up.start()
    x_down.start()
    pl.semaphore_wait(know_sem.at[1], 2)
    signal(know_sem.at[2], -4)
    signal(know_sem.at[2], 4)
    middle((1, 2))
    pl.semaphore_wait(know_sem.at[2], 2)
    signal(know_sem.at[3], -8)
    signal(know_sem.at[3], 8)
    x_up.wait_recv()
    x_down.wait_recv()

    @pl.when(me == 0)
    def _():
        xs[0] = jnp.zeros((COLS, MID), BF16)

    @pl.when(me == TILES - 1)
    def _():
        xs[ROWS + 1] = jnp.zeros((COLS, MID), BF16)

    ogain = ogain_ref[...].reshape(1, OUT)
    ogain = jnp.concatenate([ogain, ogain], axis=1)

    def upper(a, rows):
        left = jnp.concatenate(
            [jnp.concatenate([xs[h + a], xs[h + a + 1]], axis=1) for h in rows], axis=0)
        y = dot_t(left, fold[a])
        lefts = []
        for n, h in enumerate(rows):
            z = y[n * COLS:(n + 1) * COLS]
            v = (z[:, MID:] + mixed(z[:, :MID], down, up)).astype(BF16).astype(F32)
            one, two = halves_mean(v * v)
            scale = spread(lax.rsqrt(one + EPS), lax.rsqrt(two + EPS), COLS)
            normed = v * scale
            t = cotangent(normed, ogain, rewp[2 * h + a].astype(F32))
            one, two = halves_mean(t * normed)
            g = (scale * (t - normed * spread(one, two, COLS))).astype(BF16)
            lefts.append(jnp.concatenate([mixed(g.astype(F32), up, down).astype(BF16), g], axis=1))
        z = dot(jnp.concatenate(lefts, axis=0), fold[a])
        return {h: (z[n * COLS:(n + 1) * COLS, :MID], z[n * COLS:(n + 1) * COLS, MID:])
                for n, h in enumerate(rows)}

    z0 = upper(0, (0, 1))
    psend[0] = z0[0][0].astype(BF16)
    p_up = remote(psend.at[0], precv.at[1], p_send.at[0], p_recv.at[0], -1)
    p_up.start()
    z1 = upper(1, (2, 3))
    psend[1] = z1[3][1].astype(BF16)
    p_down = remote(psend.at[1], precv.at[0], p_send.at[1], p_recv.at[1], 1)
    p_down.start()
    z0.update(upper(0, (2, 3)))
    z1.update(upper(1, (0, 1)))
    p_up.wait_recv()
    p_down.wait_recv()

    @pl.when(me == 0)
    def _():
        precv[0] = jnp.zeros((COLS, MID), BF16)

    @pl.when(me == TILES - 1)
    def _():
        precv[1] = jnp.zeros((COLS, MID), BF16)

    bg[1] = (z0[0][1] + z0[1][0] + z1[0][0] + precv[0].astype(F32)).astype(BF16)
    bg[ROWS] = (z0[3][1] + precv[1].astype(F32) + z1[3][0] + z1[2][1]).astype(BF16)
    b_up = remote(bg.at[1], bg.at[ROWS + 1], b_send.at[0], b_recv.at[0], -1)
    b_down = remote(bg.at[ROWS], bg.at[0], b_send.at[1], b_recv.at[1], 1)
    b_up.start()
    b_down.start()
    for h in (1, 2):
        bg[h + 1] = (z0[h][1] + z0[h + 1][0] + z1[h][0] + z1[h - 1][1]).astype(BF16)

    for copy in load_back:
        copy.wait()

    def lower(rows):
        left = jnp.concatenate(
            [jnp.concatenate([bg[h + 2], bg[h + 1], bg[h]], axis=1) for h in rows], axis=0)
        y = dot_t(left, wback[...].reshape(3 * MID, 3 * MID))
        for n, h in enumerate(rows):
            z = y[n * COLS:(n + 1) * COLS]
            grad = z[:, MID:2 * MID] + up(z[:, :MID]) + down(z[:, 2 * MID:])
            v = hid[h + 1].astype(F32)
            scale = lax.rsqrt(jnp.mean(v * v, axis=1, keepdims=True) + EPS)
            normed = v * scale
            t = cotangent(normed, gain, grad)
            m = jnp.mean(t * normed, axis=1, keepdims=True)
            g = (bg[h + 1].astype(F32) + scale * (t - normed * m)).astype(BF16)
            last = dot_t(g, vt[(h % 2) * 512:(h % 2) * 512 + 512])
            for p in range(4):
                zs[h, p, 8:COLS + 8] = last[:, p * 128:(p + 1) * 128]

    lower((1, 2))
    b_up.wait_recv()
    b_down.wait_recv()

    @pl.when(me == 0)
    def _():
        bg[0] = jnp.zeros((COLS, MID), BF16)

    @pl.when(me == TILES - 1)
    def _():
        bg[ROWS + 1] = jnp.zeros((COLS, MID), BF16)

    lower((0, 3))

    def tokens(h):
        picks = ((0, 0), (1, 1), (2, 2), (3, -1))
        parts = [zs[h, n, pl.ds(8 + d, TOK, stride=2), :] for n, d in picks]
        return (parts[0] + parts[1]) + (parts[2] + parts[3])

    u0, u1, u2, u3 = (tokens(h) for h in range(ROWS))
    low = iota((TOK, 128), 1) < 64
    m0 = jnp.where(low, u0 + u1 + pltpu.roll(u2, 64, 1), u3)
    m1 = jnp.where(low, u2 + u3 + pltpu.roll(u1, 64, 1), u0)
    both = jnp.concatenate([m0, m1], axis=0).astype(BF16)
    row = iota((256, TILES * PIECE), 0)
    source = lax.shift_right_logical(row, 3) * PIECE + (row & 7)
    take = ((row & 7) < PIECE) & (iota((256, TILES * PIECE), 1) == source)
    blocks = dot(jnp.where(take, 1.0, 0.0).astype(BF16), both)
    tsend[...] = blocks.reshape(TILES, 8, 128).astype(BF16)

    pl.semaphore_wait(know_sem.at[3], 2)

    def block_copy(k):
        to = lax.rem(me + k, TILES)
        return pltpu.make_async_remote_copy(
            src_ref=tsend.at[to], dst_ref=trecv.at[me], send_sem=t_send.at[k],
            recv_sem=t_recv.at[k],
            device_id={"tile": to}, device_id_type=pl.DeviceIdType.MESH)

    for k in range(1, TILES):
        block_copy(k).start()
    trecv[me] = tsend[me]
    for k in range(1, TILES):
        source = lax.rem(me + (TILES - k), TILES)
        pltpu.make_async_remote_copy(
            src_ref=tsend.at[source], dst_ref=trecv.at[source], send_sem=t_send.at[k],
            recv_sem=t_recv.at[k],
            device_id={"tile": source}, device_id_type=pl.DeviceIdType.MESH).wait_recv()
    got = trecv[...].astype(F32).reshape(TILES * 8, 128).T.astype(BF16)
    out_ref[...] = dot(got[:64], place[0]) + dot(got[64:], place[1])

    for copies in halo:
        for copy in copies:
            copy.wait_send()
    for copy in (x_up, x_down, p_up, p_down, b_up, b_down):
        copy.wait_send()
    for k in range(1, TILES):
        block_copy(k).wait_send()


def shards(latent, cached_latent, cached_features, reward_grad, conv_in_weight, conv_mid_weight,
           conv_up_weight, norm_gain, out_gain, shard_order):
    hbm = pl.BlockSpec(memory_space=pltpu.HBM)
    vmem = pl.BlockSpec(memory_space=pltpu.VMEM)
    smem = pl.BlockSpec(memory_space=pltpu.SMEM)
    dma = pltpu.SemaphoreType.DMA
    call = pl.pallas_call(
        kernel,
        out_shape=jax.ShapeDtypeStruct((4 * LAT, TILES * PIECE), F32),
        in_specs=[hbm] * 7 + [vmem, vmem, smem],
        out_specs=vmem,
        scratch_shapes=[
            pltpu.VMEM((3, ROWS + 4, LAT, COLS), BF16),
            pltpu.VMEM((3, ROWS + 2, COLS, MID), BF16),
            pltpu.VMEM((ROWS + 2, COLS, MID), BF16),
            pltpu.VMEM((ROWS + 2, COLS, MID), BF16),
            pltpu.VMEM((2 * ROWS, OUT, 2 * COLS), BF16),
            pltpu.VMEM((2 * ROWS, COLS, 2 * OUT), BF16),
            pltpu.VMEM((3, 3, 3, LAT, MID), BF16),
            pltpu.VMEM((3, 3, MID, 3 * MID), BF16),
            pltpu.VMEM((3, MID, 3 * MID), BF16),
            pltpu.VMEM((3, 3, OUT, MID), BF16),
            pltpu.VMEM((2, 4 * OUT, 2 * MID), BF16),
            pltpu.VMEM((1024, MID), BF16),
            pltpu.VMEM((2, COLS, MID), BF16),
            pltpu.VMEM((2, COLS, MID), BF16),
            pltpu.VMEM((ROWS + 2, COLS, MID), BF16),
            pltpu.VMEM((ROWS, 4, COLS + 16, 128), F32),
            pltpu.VMEM((TILES, 8, 128), BF16),
            pltpu.VMEM((TILES, 8, 128), BF16),
            pltpu.VMEM((2, 256, TILES * PIECE), BF16),
            dma((18,)), dma((2, 3)), dma((2, 3)), dma((2,)), dma((2,)), dma((2,)), dma((2,)),
            dma((2,)), dma((2,)), dma((TILES,)), dma((TILES,)),
            pltpu.SemaphoreType.REGULAR((4,)),
        ],
        compiler_params=pltpu.CompilerParams(
            collective_id=0, has_side_effects=True, vmem_limit_bytes=60 << 20),
    )
    out = call(jnp.swapaxes(latent, 1, 2), jnp.swapaxes(cached_latent, 2, 3), cached_features,
               jnp.swapaxes(reward_grad, 1, 2), conv_in_weight, conv_mid_weight,
               jnp.swapaxes(conv_up_weight, 2, 3), norm_gain, out_gain, shard_order)
    return out.T


def solution(mesh):
    part = P(("prompt", "tile"), None, None)
    frames = P(None, ("prompt", "tile"), None, None)
    return jax.shard_map(
        shards,
        mesh=mesh,
        in_specs=(part, frames, frames, part, P(), P(), P(), P(), P(), P("prompt")),
        out_specs=P(("prompt", "tile"), None),
        check_vma=False,
    )
```

```python
import jax
import jax.numpy as jnp
from jax import lax
from jax.experimental import pallas as pl
from jax.experimental.pallas import tpu as pltpu
from jax.sharding import PartitionSpec as P

EPS = 1e-06
F32 = jnp.float32
BF16 = jnp.bfloat16
ROWS = 4
COLS = 160
LAT = 16
MID = 384
OUT = 192
TILES = 32
PIECE = 5
TOK = 80
VMEM_LIMIT = 60 << 20


def hops(k):
    z = (k // 2) % 8
    return min(z, 8 - z) + (1 if 8 <= k < 24 else 0)


FAR_FIRST = sorted(range(1, TILES), key=lambda k: -hops(k))


def iota(shape, dim):
    return lax.broadcasted_iota(jnp.int32, shape, dim)


def down(x):
    return jnp.where(iota(x.shape, 0) == 0, 0.0, pltpu.roll(x, 1, 0))


def up(x):
    n = x.shape[0]
    return jnp.where(iota(x.shape, 0) == n - 1, 0.0, pltpu.roll(x, n - 1, 0))


def mixed(x, low, high):
    a, b, c = x[:, :128], x[:, 128:256], x[:, 256:]
    middle = jnp.where(iota(b.shape, 1) < 64, low(b), high(b))
    return jnp.concatenate([low(a), middle, high(c)], axis=1)


def halves_mean(x):
    a, b, c = x[:, :128], x[:, 128:256], x[:, 256:]
    left = iota(b.shape, 1) < 64
    first = jnp.sum(a + jnp.where(left, b, 0.0), axis=1, keepdims=True) * (1.0 / OUT)
    second = jnp.sum(c + jnp.where(left, 0.0, b), axis=1, keepdims=True) * (1.0 / OUT)
    return first, second


def spread(first, second, rows):
    left = iota((rows, 128), 1) < 64
    one = jnp.broadcast_to(first, (rows, 128))
    two = jnp.broadcast_to(second, (rows, 128))
    return jnp.concatenate([one, jnp.where(left, one, two), two], axis=1)


def cotangent(normed, half_gain, grad):
    q = normed * half_gain
    t = jnp.tanh(q)
    return (grad * half_gain) * ((1.0 + t) * (1.0 + q * (1.0 - t)))


def dot(a, b):
    return jnp.dot(a, b, preferred_element_type=F32)


def dot_t(a, b):
    return lax.dot_general(a, b, (((1,), (1,)), ((), ())), preferred_element_type=F32)


def kernel(
    lat_in, latc_in, feat_in, rew_in, win_in, wmid_in, wup_in, gain_in, ogain_in, order_in,
    out_ref,
    lat, feat, hid, xs, rew, rewp, win, wmid, wback, wup, fold, vt,
    psend, precv, bg, zs, tsend, trecv, place, acc, gain_ref, ogain_ref, order_ref,
    local_sem, halo_send, halo_recv, x_send, x_recv, p_send, p_recv, b_send, b_recv,
    t_send, t_recv, know_sem,
):
    me = lax.axis_index("tile")

    def at(offset):
        return {"tile": lax.rem(me + (offset + TILES), TILES)}

    def signal(sem, offset):
        pl.semaphore_signal(sem, inc=1, device_id=at(offset), device_id_type=pl.DeviceIdType.MESH)

    def remote(src, dst, send, recv, offset):
        return pltpu.make_async_remote_copy(
            src_ref=src, dst_ref=dst, send_sem=send, recv_sem=recv,
            device_id=at(offset), device_id_type=pl.DeviceIdType.MESH,
        )

    local = []

    def load(src, dst):
        copy = pltpu.make_async_copy(src, dst, local_sem.at[len(local)])
        copy.start()
        local.append(copy)
        return copy

    barrier = pltpu.get_barrier_semaphore()
    signal(barrier, -1)
    signal(barrier, 1)
    load_lat = [
        load(lat_in, lat.at[2, pl.ds(2, ROWS)]),
        load(latc_in, lat.at[pl.ds(0, 2), pl.ds(2, ROWS)]),
    ]
    load_win = load(win_in, win)
    load_wup = load(wup_in, wup)
    load_rew = load(rew_in, rew)
    load_feat = load(feat_in, feat.at[pl.ds(0, 2), pl.ds(1, ROWS)])
    load_small = [load(gain_in, gain_ref), load(ogain_in, ogain_ref), load(order_in, order_ref)]
    load_mid = []
    for t in (0, 1, 2):
        for j in range(3):
            load_mid.append(load(wmid_in.at[t, :, j], wmid.at[t, :, :, pl.ds(j * MID, MID)]))
    load_back = []
    for i in range(3):
        load_back.append(load(wmid_in.at[2, i], wback.at[:, :, pl.ds(i * MID, MID)]))

    pl.semaphore_wait(barrier, 2)
    halo = []
    for side, offset in ((0, -1), (1, 1)):
        row = 0 if side == 0 else ROWS - 2
        land = ROWS + 2 if side == 0 else 0
        copies = [
            remote(lat_in.at[pl.ds(row, 2)], lat.at[2, pl.ds(land, 2)],
                   halo_send.at[side, 0], halo_recv.at[side, 0], offset),
            remote(latc_in.at[:, pl.ds(row, 2)], lat.at[pl.ds(0, 2), pl.ds(land, 2)],
                   halo_send.at[side, 1], halo_recv.at[side, 1], offset),
        ]
        row = 0 if side == 0 else ROWS - 1
        land = ROWS + 1 if side == 0 else 0
        copies.append(
            remote(feat_in.at[:, pl.ds(row, 1)], feat.at[pl.ds(0, 2), pl.ds(land, 1)],
                   halo_send.at[side, 2], halo_recv.at[side, 2], offset))
        halo.append(copies)
    for n in range(3):
        for side in range(2):
            halo[side][n].start()
    signal(know_sem.at[0], -1)
    signal(know_sem.at[0], 1)

    load_wup.wait()
    parts = []
    for i in range(3):
        k0, k1, k2 = (wup[i, j].astype(F32) for j in range(3))
        parts.append(jnp.concatenate([k0, k2, k1 + k2, k0 + k1], axis=0))
    fold[0, :, :MID] = parts[0].astype(BF16)
    fold[0, :, MID:] = (parts[1] + parts[2]).astype(BF16)
    fold[1, :, :MID] = (parts[0] + parts[1]).astype(BF16)
    fold[1, :, MID:] = parts[2].astype(BF16)

    load_rew.wait()
    n = iota((2 * COLS, 2 * COLS), 0)
    column = jnp.where(n < COLS, 2 * n, 2 * n - (2 * COLS - 1))
    parting = jnp.where(iota((2 * COLS, 2 * COLS), 1) == column, 1.0, 0.0).astype(BF16)
    left = iota((COLS, 128), 1) < 64
    for y in range(2 * ROWS):
        flat = jnp.concatenate([rew[y], jnp.zeros((256 - OUT, 2 * COLS), BF16)], axis=0)
        parted = dot_t(parting, flat)
        even, odd = parted[:COLS], parted[COLS:]
        o0, o1 = pltpu.roll(odd[:, :128], 64, 1), pltpu.roll(odd[:, 128:], 64, 1)
        rewp[y] = jnp.concatenate(
            [even[:, :128], jnp.where(left, even[:, 128:], o0), jnp.where(left, o0, o1)],
            axis=1).astype(BF16)

    for copy in load_lat + load_mid[:3] + [load_win, load_feat] + load_small:
        copy.wait()
    for n in range(2):
        for side in range(2):
            halo[side][n].wait_recv()

    @pl.when(me == 0)
    def _():
        lat[:, 0:2] = jnp.zeros((3, 2, LAT, COLS), BF16)

    @pl.when(me == TILES - 1)
    def _():
        lat[:, ROWS + 2:] = jnp.zeros((3, 2, LAT, COLS), BF16)

    def frames(rows, times):
        return jnp.concatenate(
            [jnp.concatenate([feat[t, h + i] for t in times for i in range(3)], axis=1)
             for h in rows], axis=0)

    taps = []
    for h in range(ROWS + 4):
        x = jnp.concatenate([lat[t, h].astype(F32) for t in range(3)], axis=0).T
        taps.append(jnp.concatenate([down(x), x, up(x)], axis=1).astype(BF16))
    total = None
    for i in range(3):
        weight = jnp.concatenate([win[t, i, j] for j in range(3) for t in range(3)], axis=0)
        part = dot(jnp.concatenate(taps[i:i + ROWS + 2], axis=0), weight)
        total = part if total is None else total + part
    acc[...] = dot(frames((1, 2), (0,)), wmid[0].reshape(3 * MID, 3 * MID))
    half_gain = gain_ref[...].reshape(1, MID) * 0.5
    for h in range(ROWS + 2):
        value = total[h * COLS:(h + 1) * COLS].astype(BF16)
        hid[h] = value
        v = value.astype(F32)
        q = v * lax.rsqrt(jnp.mean(v * v, axis=1, keepdims=True) + EPS) * half_gain
        feat[2, h] = (q + q * jnp.tanh(q)).astype(BF16)

    for side in range(2):
        halo[side][2].wait_recv()

    @pl.when(me == 0)
    def _():
        feat[:, 0] = jnp.zeros((3, COLS, MID), BF16)

    @pl.when(me == TILES - 1)
    def _():
        feat[:, ROWS + 1] = jnp.zeros((3, COLS, MID), BF16)

    for copy in load_mid[3:]:
        copy.wait()
    pl.semaphore_wait(know_sem.at[0], 2)
    signal(know_sem.at[1], -2)
    signal(know_sem.at[1], 2)

    def middle(rows, times, start=None):
        depth = 3 * MID * len(times)
        y = dot(frames(rows, times), wmid[times[0]:].reshape(depth, 3 * MID))
        if start is not None:
            y = y + start[...]
        for n, h in enumerate(rows):
            z = y[n * COLS:(n + 1) * COLS]
            value = z[:, MID:2 * MID] + down(z[:, :MID]) + up(z[:, 2 * MID:])
            xs[h + 1] = (hid[h + 1].astype(F32) + value).astype(BF16)

    middle((0, 3), (0, 1, 2))
    x_up = remote(xs.at[1], xs.at[ROWS + 1], x_send.at[0], x_recv.at[0], -1)
    x_down = remote(xs.at[ROWS], xs.at[0], x_send.at[1], x_recv.at[1], 1)
    x_up.start()
    x_down.start()
    pl.semaphore_wait(know_sem.at[1], 2)
    signal(know_sem.at[2], -4)
    signal(know_sem.at[2], 4)
    middle((1, 2), (1, 2), acc)
    pl.semaphore_wait(know_sem.at[2], 2)
    signal(know_sem.at[3], -8)
    signal(know_sem.at[3], 8)
    x_up.wait_recv()
    x_down.wait_recv()

    @pl.when(me == 0)
    def _():
        xs[0] = jnp.zeros((COLS, MID), BF16)

    @pl.when(me == TILES - 1)
    def _():
        xs[ROWS + 1] = jnp.zeros((COLS, MID), BF16)

    half_ogain = ogain_ref[...].reshape(1, OUT) * 0.5
    half_ogain = jnp.concatenate([half_ogain, half_ogain], axis=1)

    def forward(a, rows):
        left = jnp.concatenate(
            [jnp.concatenate([xs[h + a], xs[h + a + 1]], axis=1) for h in rows], axis=0)
        return dot_t(left, fold[a])

    def pull(a, rows, y):
        lefts = []
        for n, h in enumerate(rows):
            z = y[n * COLS:(n + 1) * COLS]
            v = (z[:, MID:] + mixed(z[:, :MID], down, up)).astype(BF16).astype(F32)
            one, two = halves_mean(v * v)
            scale = spread(lax.rsqrt(one + EPS), lax.rsqrt(two + EPS), COLS)
            normed = v * scale
            t = cotangent(normed, half_ogain, rewp[2 * h + a].astype(F32))
            one, two = halves_mean(t * normed)
            g = scale * (t - normed * spread(one, two, COLS))
            lefts.append(jnp.concatenate([mixed(g, up, down), g], axis=1).astype(BF16))
        return jnp.concatenate(lefts, axis=0)

    def back(a, rows, left):
        z = dot(left, fold[a])
        return {h: (z[n * COLS:(n + 1) * COLS, :MID], z[n * COLS:(n + 1) * COLS, MID:])
                for n, h in enumerate(rows)}

    batches = ((0, (0, 1)), (1, (2, 3)), (0, (2, 3)), (1, (0, 1)))
    zz = [{}, {}]
    sent = []
    y = forward(*batches[0])
    for n, (a, rows) in enumerate(batches):
        following = forward(*batches[n + 1]) if n < 3 else None
        zz[a].update(back(a, rows, pull(a, rows, y)))
        y = following
        if n < 2:
            psend[n] = (zz[0][0][0] if n == 0 else zz[1][3][1]).astype(BF16)
            copy = remote(psend.at[n], precv.at[1 - n], p_send.at[n], p_recv.at[n], 2 * n - 1)
            copy.start()
            sent.append(copy)
    z0, z1 = zz
    p_up, p_down = sent
    p_up.wait_recv()
    p_down.wait_recv()

    @pl.when(me == 0)
    def _():
        precv[0] = jnp.zeros((COLS, MID), BF16)

    @pl.when(me == TILES - 1)
    def _():
        precv[1] = jnp.zeros((COLS, MID), BF16)

    bg[1] = (z0[0][1] + z0[1][0] + z1[0][0] + precv[0].astype(F32)).astype(BF16)
    bg[ROWS] = (z0[3][1] + precv[1].astype(F32) + z1[3][0] + z1[2][1]).astype(BF16)
    b_up = remote(bg.at[1], bg.at[ROWS + 1], b_send.at[0], b_recv.at[0], -1)
    b_down = remote(bg.at[ROWS], bg.at[0], b_send.at[1], b_recv.at[1], 1)
    b_up.start()
    b_down.start()
    for h in (1, 2):
        bg[h + 1] = (z0[h][1] + z0[h + 1][0] + z1[h][0] + z1[h - 1][1]).astype(BF16)

    r = iota((1024, 144), 0)
    par = lax.shift_right_logical(r, 9)
    d = lax.shift_right_logical(r, 7) & 3
    d = jnp.where(d == 3, -1, d)
    extra = lax.shift_right_logical(r, 6) & 1
    a = lax.shift_right_logical(r, 5) & 1
    b = lax.shift_right_logical(r, 4) & 1
    c = r & 15
    i = jnp.where(extra == 0, jnp.where(par == 0, a + 1, a), jnp.where(par == 0, 0, 2))
    fits = jnp.where(extra == 0, 1, jnp.where(par == 0, a, 1 - a))
    j = b - d + 1
    fits = jnp.where((j >= 0) & (j <= 2), fits, 0)
    want = jnp.where(fits == 1, i * 48 + j * 16 + c, -1)
    pick = jnp.where(iota((1024, 144), 1) == want, 1.0, 0.0).astype(BF16)
    vt[...] = dot(pick, win[2].reshape(144, MID)).astype(BF16)
    zs[:, :, 0:8] = jnp.zeros((ROWS, 4, 8, 128), F32)
    zs[:, :, COLS + 8:] = jnp.zeros((ROWS, 4, 8, 128), F32)

    for copy in load_back:
        copy.wait()

    def lower(rows):
        left = jnp.concatenate(
            [jnp.concatenate([bg[h + 2], bg[h + 1], bg[h]], axis=1) for h in rows], axis=0)
        y = dot_t(left, wback[...].reshape(3 * MID, 3 * MID))
        for n, h in enumerate(rows):
            z = y[n * COLS:(n + 1) * COLS]
            grad = z[:, MID:2 * MID] + up(z[:, :MID]) + down(z[:, 2 * MID:])
            v = hid[h + 1].astype(F32)
            scale = lax.rsqrt(jnp.mean(v * v, axis=1, keepdims=True) + EPS)
            normed = v * scale
            t = cotangent(normed, half_gain, grad)
            m = jnp.mean(t * normed, axis=1, keepdims=True)
            g = (bg[h + 1].astype(F32) + scale * (t - normed * m)).astype(BF16)
            last = dot_t(g, vt[(h % 2) * 512:(h % 2) * 512 + 512])
            for p in range(4):
                zs[h, p, 8:COLS + 8] = last[:, p * 128:(p + 1) * 128]

    lower((1, 2))
    b_up.wait_recv()
    b_down.wait_recv()

    @pl.when(me == 0)
    def _():
        bg[0] = jnp.zeros((COLS, MID), BF16)

    @pl.when(me == TILES - 1)
    def _():
        bg[ROWS + 1] = jnp.zeros((COLS, MID), BF16)

    lower((0, 3))

    def tokens(h):
        picks = ((0, 0), (1, 1), (2, 2), (3, -1))
        parts = [zs[h, n, pl.ds(8 + d, TOK, stride=2), :] for n, d in picks]
        return (parts[0] + parts[1]) + (parts[2] + parts[3])

    u0, u1, u2, u3 = (tokens(h) for h in range(ROWS))
    low = iota((TOK, 128), 1) < 64
    m0 = jnp.where(low, u0 + u1 + pltpu.roll(u2, 64, 1), u3)
    m1 = jnp.where(low, u2 + u3 + pltpu.roll(u1, 64, 1), u0)
    both = jnp.concatenate([m0, m1], axis=0).astype(BF16)
    row = iota((256, TILES * PIECE), 0)
    source = lax.shift_right_logical(row, 3) * PIECE + (row & 7)
    take = ((row & 7) < PIECE) & (iota((256, TILES * PIECE), 1) == source)
    blocks = dot(jnp.where(take, 1.0, 0.0).astype(BF16), both)
    tsend[...] = blocks.reshape(TILES, 8, 128).astype(BF16)

    pl.semaphore_wait(know_sem.at[3], 2)

    def block_copy(k):
        to = lax.rem(me + k, TILES)
        return pltpu.make_async_remote_copy(
            src_ref=tsend.at[to], dst_ref=trecv.at[me], send_sem=t_send.at[k],
            recv_sem=t_recv.at[k],
            device_id={"tile": to}, device_id_type=pl.DeviceIdType.MESH)

    for k in FAR_FIRST:
        block_copy(k).start()
    trecv[me] = tsend[me]

    slot = lax.shift_right_logical(iota((256, 1), 0), 3)
    own_at = jnp.full((256, 1), -1, jnp.int32)
    edge_at = jnp.full((256, 1), -1, jnp.int32)
    for t in range(TILES):
        own_at = jnp.where(slot == t, order_ref[t], own_at)
        after = order_ref[t + 1] if t + 1 < TILES else jnp.int32(-1)
        before = order_ref[t - 1] if t > 0 else jnp.int32(-1)
        edge_at = jnp.where(slot == t, jnp.where(me < TILES // 2, after, before), edge_at)
    spot = iota((256, TILES * PIECE), 1)
    block = lax.shift_right_logical(spot * 205, 10)
    same = (spot - block * PIECE) == (iota((256, TILES * PIECE), 0) & 7)
    place[0] = jnp.where(same & (block == own_at), 1.0, 0.0).astype(BF16)
    place[1] = jnp.where(same & (block == edge_at), 1.0, 0.0).astype(BF16)

    for k in range(1, TILES):
        source = lax.rem(me + (TILES - k), TILES)
        pltpu.make_async_remote_copy(
            src_ref=tsend.at[source], dst_ref=trecv.at[source], send_sem=t_send.at[k],
            recv_sem=t_recv.at[k],
            device_id={"tile": source}, device_id_type=pl.DeviceIdType.MESH).wait_recv()
    got = trecv[...].astype(F32).reshape(TILES * 8, 128).T.astype(BF16)
    out_ref[...] = dot(got[:64], place[0]) + dot(got[64:], place[1])

    for copies in halo:
        for copy in copies:
            copy.wait_send()
    for copy in (x_up, x_down, p_up, p_down, b_up, b_down):
        copy.wait_send()
    for k in range(1, TILES):
        block_copy(k).wait_send()


def shards(latent, cached_latent, cached_features, reward_grad, conv_in_weight, conv_mid_weight,
           conv_up_weight, norm_gain, out_gain, shard_order):
    hbm = pl.BlockSpec(memory_space=pltpu.HBM)
    dma = pltpu.SemaphoreType.DMA
    call = pl.pallas_call(
        kernel,
        out_shape=pltpu.VMEM((4 * LAT, TILES * PIECE), F32),
        in_specs=[hbm] * 10,
        out_specs=pl.BlockSpec(memory_space=pltpu.VMEM),
        scratch_shapes=[
            pltpu.VMEM((3, ROWS + 4, LAT, COLS), BF16),
            pltpu.VMEM((3, ROWS + 2, COLS, MID), BF16),
            pltpu.VMEM((ROWS + 2, COLS, MID), BF16),
            pltpu.VMEM((ROWS + 2, COLS, MID), BF16),
            pltpu.VMEM((2 * ROWS, OUT, 2 * COLS), BF16),
            pltpu.VMEM((2 * ROWS, COLS, 2 * OUT), BF16),
            pltpu.VMEM((3, 3, 3, LAT, MID), BF16),
            pltpu.VMEM((3, 3, MID, 3 * MID), BF16),
            pltpu.VMEM((3, MID, 3 * MID), BF16),
            pltpu.VMEM((3, 3, OUT, MID), BF16),
            pltpu.VMEM((2, 4 * OUT, 2 * MID), BF16),
            pltpu.VMEM((1024, MID), BF16),
            pltpu.VMEM((2, COLS, MID), BF16),
            pltpu.VMEM((2, COLS, MID), BF16),
            pltpu.VMEM((ROWS + 2, COLS, MID), BF16),
            pltpu.VMEM((ROWS, 4, COLS + 16, 128), F32),
            pltpu.VMEM((TILES, 8, 128), BF16),
            pltpu.VMEM((TILES, 8, 128), BF16),
            pltpu.VMEM((2, 256, TILES * PIECE), BF16),
            pltpu.VMEM((2 * COLS, 3 * MID), F32),
            pltpu.VMEM((MID,), F32), pltpu.VMEM((OUT,), F32), pltpu.SMEM((TILES,), jnp.int32),
            dma((24,)), dma((2, 3)), dma((2, 3)), dma((2,)), dma((2,)), dma((2,)), dma((2,)),
            dma((2,)), dma((2,)), dma((TILES,)), dma((TILES,)),
            pltpu.SemaphoreType.REGULAR((4,)),
        ],
        compiler_params=pltpu.CompilerParams(
            collective_id=0, has_side_effects=True, vmem_limit_bytes=VMEM_LIMIT),
    )
    out = call(jnp.swapaxes(latent, 1, 2), jnp.swapaxes(cached_latent, 2, 3), cached_features,
               jnp.swapaxes(reward_grad, 1, 2), conv_in_weight, conv_mid_weight,
               jnp.swapaxes(conv_up_weight, 2, 3), norm_gain, out_gain, shard_order)
    return out.T


def solution(mesh):
    part = P(("prompt", "tile"), None, None)
    frames = P(None, ("prompt", "tile"), None, None)
    return jax.shard_map(
        shards,
        mesh=mesh,
        in_specs=(part, frames, frames, part, P(), P(), P(), P(), P(), P("prompt")),
        out_specs=P(("prompt", "tile"), None),
        check_vma=False,
    )
```

```python
import jax
import jax.numpy as jnp
from jax import lax
from jax.experimental import pallas as pl
from jax.experimental.pallas import tpu as pltpu
from jax.sharding import PartitionSpec as P

EPS = 1e-06
F32 = jnp.float32
BF16 = jnp.bfloat16
ROWS = 4
COLS = 160
LAT = 16
MID = 384
OUT = 192
TILES = 32
PIECE = 5
TOK = 80
CHUNKS = ((0, 256), (256, 128))
VMEM_LIMIT = 60 << 20


def hops(k):
    z = (k // 2) % 8
    return min(z, 8 - z) + (1 if 8 <= k < 24 else 0)


FAR_FIRST = sorted(range(1, TILES), key=lambda k: -hops(k))


def iota(shape, dim):
    return lax.broadcasted_iota(jnp.int32, shape, dim)


def down(x):
    return jnp.where(iota(x.shape, 0) == 0, 0.0, pltpu.roll(x, 1, 0))


def up(x):
    n = x.shape[0]
    return jnp.where(iota(x.shape, 0) == n - 1, 0.0, pltpu.roll(x, n - 1, 0))


def mixed(x, low, high):
    a, b, c = x[:, :128], x[:, 128:256], x[:, 256:]
    middle = jnp.where(iota(b.shape, 1) < 64, low(b), high(b))
    return jnp.concatenate([low(a), middle, high(c)], axis=1)


def halves_mean(x):
    a, b, c = x[:, :128], x[:, 128:256], x[:, 256:]
    left = iota(b.shape, 1) < 64
    first = jnp.sum(a + jnp.where(left, b, 0.0), axis=1, keepdims=True) * (1.0 / OUT)
    second = jnp.sum(c + jnp.where(left, 0.0, b), axis=1, keepdims=True) * (1.0 / OUT)
    return first, second


def spread(first, second, rows):
    left = iota((rows, 128), 1) < 64
    one = jnp.broadcast_to(first, (rows, 128))
    two = jnp.broadcast_to(second, (rows, 128))
    return jnp.concatenate([one, jnp.where(left, one, two), two], axis=1)


def cotangent(normed, half_gain, grad):
    q = normed * half_gain
    t = jnp.tanh(q)
    return (grad * half_gain) * ((1.0 + t) * (1.0 + q * (1.0 - t)))


def dot(a, b):
    return jnp.dot(a, b, preferred_element_type=F32)


def dot_t(a, b):
    return lax.dot_general(a, b, (((1,), (1,)), ((), ())), preferred_element_type=F32)


def kernel(
    lat_in, latc_in, feat_in, rew_in, win_in, wmid_in, wup_in, gain_in, ogain_in, order_in,
    out_ref,
    lat, feat, hid, xs, rew, rewp, win, wmid, wback, wup, fold, vt,
    bg, zs, tsend, trecv, place, acc, gain_ref, ogain_ref, order_ref,
    local_sem, halo_send, halo_recv, x_send, x_recv, b_send, b_recv,
    t_send, t_recv, know_sem,
):
    me = lax.axis_index("tile")

    def at(offset):
        return {"tile": lax.rem(me + (offset + TILES), TILES)}

    def signal(sem, offset):
        pl.semaphore_signal(sem, inc=1, device_id=at(offset), device_id_type=pl.DeviceIdType.MESH)

    def remote(src, dst, send, recv, offset):
        return pltpu.make_async_remote_copy(
            src_ref=src, dst_ref=dst, send_sem=send, recv_sem=recv,
            device_id=at(offset), device_id_type=pl.DeviceIdType.MESH,
        )

    local = []

    def load(src, dst):
        copy = pltpu.make_async_copy(src, dst, local_sem.at[len(local)])
        copy.start()
        local.append(copy)
        return copy

    barrier = pltpu.get_barrier_semaphore()
    signal(barrier, -1)
    signal(barrier, 1)
    load_lat = [
        load(lat_in, lat.at[2, pl.ds(2, ROWS)]),
        load(latc_in, lat.at[pl.ds(0, 2), pl.ds(2, ROWS)]),
    ]
    load_win = load(win_in, win)
    load_wup = load(wup_in, wup)
    load_rew = load(rew_in, rew.at[pl.ds(1, 2 * ROWS)])
    load_feat = load(feat_in, feat.at[pl.ds(0, 2), pl.ds(1, ROWS)])
    load_small = [load(gain_in, gain_ref), load(ogain_in, ogain_ref), load(order_in, order_ref)]
    load_mid = []
    for t in (0, 1, 2):
        for j in range(3):
            for start, width in CHUNKS:
                load_mid.append(load(
                    wmid_in.at[t, :, j, :, pl.ds(start, width)],
                    wmid.at[t, :, :, pl.ds(3 * start + j * width, width)]))
    pl.semaphore_wait(barrier, 2)
    halo = []
    for side, offset in ((0, -1), (1, 1)):
        row = 0 if side == 0 else ROWS - 2
        land = ROWS + 2 if side == 0 else 0
        copies = [
            remote(lat_in.at[pl.ds(row, 2)], lat.at[2, pl.ds(land, 2)],
                   halo_send.at[side, 0], halo_recv.at[side, 0], offset),
            remote(latc_in.at[:, pl.ds(row, 2)], lat.at[pl.ds(0, 2), pl.ds(land, 2)],
                   halo_send.at[side, 1], halo_recv.at[side, 1], offset),
        ]
        row = 0 if side == 0 else ROWS - 1
        land = ROWS + 1 if side == 0 else 0
        copies.append(
            remote(feat_in.at[:, pl.ds(row, 1)], feat.at[pl.ds(0, 2), pl.ds(land, 1)],
                   halo_send.at[side, 2], halo_recv.at[side, 2], offset))
        row = 0 if side == 0 else 2 * ROWS - 1
        land = 2 * ROWS + 1 if side == 0 else 0
        copies.append(
            remote(rew_in.at[pl.ds(row, 1)], rew.at[pl.ds(land, 1)],
                   halo_send.at[side, 3], halo_recv.at[side, 3], offset))
        halo.append(copies)
    for n in range(4):
        for side in range(2):
            halo[side][n].start()
    signal(know_sem.at[0], -1)
    signal(know_sem.at[0], 1)

    load_wup.wait()
    parts = []
    for i in range(3):
        k0, k1, k2 = (wup[i, j].astype(F32) for j in range(3))
        parts.append(jnp.concatenate([k0, k2, k1 + k2, k0 + k1], axis=0))
    fold[0, :, :MID] = parts[0].astype(BF16)
    fold[0, :, MID:] = (parts[1] + parts[2]).astype(BF16)
    fold[1, :, :MID] = (parts[0] + parts[1]).astype(BF16)
    fold[1, :, MID:] = parts[2].astype(BF16)

    load_rew.wait()
    n = iota((2 * COLS, 2 * COLS), 0)
    column = jnp.where(n < COLS, 2 * n, 2 * n - (2 * COLS - 1))
    parting = jnp.where(iota((2 * COLS, 2 * COLS), 1) == column, 1.0, 0.0).astype(BF16)
    left = iota((COLS, 128), 1) < 64

    def part_columns(ys):
        for y in ys:
            flat = jnp.concatenate([rew[y], jnp.zeros((256 - OUT, 2 * COLS), BF16)], axis=0)
            parted = dot_t(parting, flat)
            even, odd = parted[:COLS], parted[COLS:]
            o0, o1 = pltpu.roll(odd[:, :128], 64, 1), pltpu.roll(odd[:, 128:], 64, 1)
            rewp[y] = jnp.concatenate(
                [even[:, :128], jnp.where(left, even[:, 128:], o0), jnp.where(left, o0, o1)],
                axis=1).astype(BF16)

    part_columns(range(1, 2 * ROWS + 1))

    for copy in load_lat + load_mid[:6] + [load_win, load_feat] + load_small:
        copy.wait()
    for n in range(2):
        for side in range(2):
            halo[side][n].wait_recv()

    @pl.when(me == 0)
    def _():
        lat[:, 0:2] = jnp.zeros((3, 2, LAT, COLS), BF16)

    @pl.when(me == TILES - 1)
    def _():
        lat[:, ROWS + 2:] = jnp.zeros((3, 2, LAT, COLS), BF16)

    def frames(rows, times):
        return jnp.concatenate(
            [jnp.concatenate([feat[t, h + i] for t in times for i in range(3)], axis=1)
             for h in rows], axis=0)

    taps = []
    for h in range(ROWS + 4):
        x = jnp.concatenate([lat[t, h].astype(F32) for t in range(3)], axis=0).T
        taps.append(jnp.concatenate([down(x), x, up(x)], axis=1).astype(BF16))
    total = None
    for i in range(3):
        weight = jnp.concatenate([win[t, i, j] for j in range(3) for t in range(3)], axis=0)
        part = dot(jnp.concatenate(taps[i:i + ROWS + 2], axis=0), weight)
        total = part if total is None else total + part
    acc[...] = dot(frames((1, 2), (0,)), wmid[0].reshape(3 * MID, 3 * MID))
    half_gain = gain_ref[...].reshape(1, MID) * 0.5
    for h in range(ROWS + 2):
        value = total[h * COLS:(h + 1) * COLS].astype(BF16)
        hid[h] = value
        v = value.astype(F32)
        q = v * lax.rsqrt(jnp.mean(v * v, axis=1, keepdims=True) + EPS) * half_gain
        feat[2, h] = (q + q * jnp.tanh(q)).astype(BF16)

    for side in range(2):
        halo[side][2].wait_recv()

    @pl.when(me == 0)
    def _():
        feat[:, 0] = jnp.zeros((3, COLS, MID), BF16)

    @pl.when(me == TILES - 1)
    def _():
        feat[:, ROWS + 1] = jnp.zeros((3, COLS, MID), BF16)

    for copy in load_mid[6:]:
        copy.wait()
    load_back = []
    for i in range(3):
        load_back.append(load(wmid_in.at[2, i], wback.at[:, :, pl.ds(i * MID, MID)]))
    pl.semaphore_wait(know_sem.at[0], 2)
    signal(know_sem.at[1], -2)
    signal(know_sem.at[1], 2)

    def middle(rows, times, chunk, first=None):
        start, width = chunk
        depth = 3 * MID * len(times)
        lanes = slice(3 * start, 3 * (start + width))
        y = dot(frames(rows, times), wmid[times[0]:, :, :, lanes].reshape(depth, 3 * width))
        if first is not None:
            y = y + first[:, lanes]
        for n, h in enumerate(rows):
            z = y[n * COLS:(n + 1) * COLS]
            value = z[:, width:2 * width] + down(z[:, :width]) + up(z[:, 2 * width:])
            held = hid[h + 1, :, start:start + width].astype(F32)
            xs[h + 1, :, start:start + width] = (held + value).astype(BF16)

    x_copies = []
    for n, (start, width) in enumerate(CHUNKS):
        middle((0, 3), (0, 1, 2), (start, width))
        part = pl.ds(start, width)
        x_copies.append(remote(xs.at[1, :, part], xs.at[ROWS + 1, :, part],
                               x_send.at[n, 0], x_recv.at[n, 0], -1))
        x_copies.append(remote(xs.at[ROWS, :, part], xs.at[0, :, part],
                               x_send.at[n, 1], x_recv.at[n, 1], 1))
        x_copies[-2].start()
        x_copies[-1].start()
    for chunk in CHUNKS:
        middle((1, 2), (1, 2), chunk, acc)
    pl.semaphore_wait(know_sem.at[1], 2)
    signal(know_sem.at[2], -4)
    signal(know_sem.at[2], 4)
    half_ogain = ogain_ref[...].reshape(1, OUT) * 0.5
    half_ogain = jnp.concatenate([half_ogain, half_ogain], axis=1)

    def forward(a, rows):
        left = jnp.concatenate(
            [jnp.concatenate([xs[h + a], xs[h + a + 1]], axis=1) for h in rows], axis=0)
        return dot_t(left, fold[a])

    def pull(a, rows, y):
        lefts = []
        for n, h in enumerate(rows):
            z = y[n * COLS:(n + 1) * COLS]
            v = (z[:, MID:] + mixed(z[:, :MID], down, up)).astype(BF16).astype(F32)
            one, two = halves_mean(v * v)
            scale = spread(lax.rsqrt(one + EPS), lax.rsqrt(two + EPS), COLS)
            normed = v * scale
            t = cotangent(normed, half_ogain, rewp[2 * h + a + 1].astype(F32))
            one, two = halves_mean(t * normed)
            g = scale * (t - normed * spread(one, two, COLS))
            lefts.append(jnp.concatenate([mixed(g, up, down), g], axis=1).astype(BF16))
        return jnp.concatenate(lefts, axis=0)

    z0, z1 = zz = [{}, {}]

    def back(a, rows, left):
        z = dot(left, fold[a])
        for n, h in enumerate(rows):
            z_row = z[n * COLS:(n + 1) * COLS]
            zz[a][h] = (z_row[:, :MID], z_row[:, MID:])

    y0 = forward(0, (1, 3))
    y1 = forward(1, (0, 2))
    back(0, (1, 3), pull(0, (1, 3), y0))
    back(1, (0, 2), pull(1, (0, 2), y1))
    for side in range(2):
        halo[side][3].wait_recv()

    @pl.when(me == 0)
    def _():
        rew[0] = jnp.zeros((OUT, 2 * COLS), BF16)

    @pl.when(me == TILES - 1)
    def _():
        rew[2 * ROWS + 1] = jnp.zeros((OUT, 2 * COLS), BF16)

    part_columns((0, 2 * ROWS + 1))
    for copy in x_copies:
        copy.wait_recv()

    @pl.when(me == 0)
    def _():
        xs[0] = jnp.zeros((COLS, MID), BF16)

    @pl.when(me == TILES - 1)
    def _():
        xs[ROWS + 1] = jnp.zeros((COLS, MID), BF16)

    y1 = forward(1, (-1, 3))
    y0 = forward(0, (0, 4))
    left1 = pull(1, (-1, 3), y1)
    first = z0[1][0] + z1[0][0] + dot(left1[:COLS], fold[1, :, MID:])
    last = z0[3][1] + z1[2][1] + dot(left1[COLS:], fold[1, :, :MID])
    left0 = pull(0, (0, 4), y0)
    bg[1] = (first + dot(left0[:COLS], fold[0, :, MID:])).astype(BF16)
    bg[ROWS] = (last + dot(left0[COLS:], fold[0, :, :MID])).astype(BF16)
    b_up = remote(bg.at[1], bg.at[ROWS + 1], b_send.at[0], b_recv.at[0], -1)
    b_down = remote(bg.at[ROWS], bg.at[0], b_send.at[1], b_recv.at[1], 1)
    b_up.start()
    b_down.start()
    pl.semaphore_wait(know_sem.at[2], 2)
    signal(know_sem.at[3], -8)
    signal(know_sem.at[3], 8)
    y0 = forward(0, (2,))
    y1 = forward(1, (1,))
    back(0, (2,), pull(0, (2,), y0))
    back(1, (1,), pull(1, (1,), y1))
    for h in (1, 2):
        bg[h + 1] = (z0[h][1] + z0[h + 1][0] + z1[h][0] + z1[h - 1][1]).astype(BF16)

    r = iota((1024, 144), 0)
    par = lax.shift_right_logical(r, 9)
    d = lax.shift_right_logical(r, 7) & 3
    d = jnp.where(d == 3, -1, d)
    extra = lax.shift_right_logical(r, 6) & 1
    a = lax.shift_right_logical(r, 5) & 1
    b = lax.shift_right_logical(r, 4) & 1
    c = r & 15
    i = jnp.where(extra == 0, jnp.where(par == 0, a + 1, a), jnp.where(par == 0, 0, 2))
    fits = jnp.where(extra == 0, 1, jnp.where(par == 0, a, 1 - a))
    j = b - d + 1
    fits = jnp.where((j >= 0) & (j <= 2), fits, 0)
    want = jnp.where(fits == 1, i * 48 + j * 16 + c, -1)
    pick = jnp.where(iota((1024, 144), 1) == want, 1.0, 0.0).astype(BF16)
    vt[...] = dot(pick, win[2].reshape(144, MID)).astype(BF16)
    zs[:, :, 0:8] = jnp.zeros((ROWS, 4, 8, 128), F32)
    zs[:, :, COLS + 8:] = jnp.zeros((ROWS, 4, 8, 128), F32)

    for copy in load_back:
        copy.wait()

    def lower(rows):
        left = jnp.concatenate(
            [jnp.concatenate([bg[h + 2], bg[h + 1], bg[h]], axis=1) for h in rows], axis=0)
        y = dot_t(left, wback[...].reshape(3 * MID, 3 * MID))
        for n, h in enumerate(rows):
            z = y[n * COLS:(n + 1) * COLS]
            grad = z[:, MID:2 * MID] + up(z[:, :MID]) + down(z[:, 2 * MID:])
            v = hid[h + 1].astype(F32)
            scale = lax.rsqrt(jnp.mean(v * v, axis=1, keepdims=True) + EPS)
            normed = v * scale
            t = cotangent(normed, half_gain, grad)
            m = jnp.mean(t * normed, axis=1, keepdims=True)
            g = (bg[h + 1].astype(F32) + scale * (t - normed * m)).astype(BF16)
            last = dot_t(g, vt[(h % 2) * 512:(h % 2) * 512 + 512])
            for p in range(4):
                zs[h, p, 8:COLS + 8] = last[:, p * 128:(p + 1) * 128]

    lower((1, 2))
    b_up.wait_recv()
    b_down.wait_recv()

    @pl.when(me == 0)
    def _():
        bg[0] = jnp.zeros((COLS, MID), BF16)

    @pl.when(me == TILES - 1)
    def _():
        bg[ROWS + 1] = jnp.zeros((COLS, MID), BF16)

    lower((0, 3))

    def tokens(h):
        picks = ((0, 0), (1, 1), (2, 2), (3, -1))
        parts = [zs[h, n, pl.ds(8 + d, TOK, stride=2), :] for n, d in picks]
        return (parts[0] + parts[1]) + (parts[2] + parts[3])

    u0, u1, u2, u3 = (tokens(h) for h in range(ROWS))
    low = iota((TOK, 128), 1) < 64
    m0 = jnp.where(low, u0 + u1 + pltpu.roll(u2, 64, 1), u3)
    m1 = jnp.where(low, u2 + u3 + pltpu.roll(u1, 64, 1), u0)
    both = jnp.concatenate([m0, m1], axis=0).astype(BF16)
    row = iota((256, TILES * PIECE), 0)
    source = lax.shift_right_logical(row, 3) * PIECE + (row & 7)
    take = ((row & 7) < PIECE) & (iota((256, TILES * PIECE), 1) == source)
    blocks = dot(jnp.where(take, 1.0, 0.0).astype(BF16), both)
    tsend[...] = blocks.reshape(TILES, 8, 128).astype(BF16)

    pl.semaphore_wait(know_sem.at[3], 2)

    def block_copy(k):
        to = lax.rem(me + k, TILES)
        return pltpu.make_async_remote_copy(
            src_ref=tsend.at[to], dst_ref=trecv.at[me], send_sem=t_send.at[k],
            recv_sem=t_recv.at[k],
            device_id={"tile": to}, device_id_type=pl.DeviceIdType.MESH)

    for k in FAR_FIRST:
        block_copy(k).start()
    trecv[me] = tsend[me]

    slot = lax.shift_right_logical(iota((256, 1), 0), 3)
    own_at = jnp.full((256, 1), -1, jnp.int32)
    edge_at = jnp.full((256, 1), -1, jnp.int32)
    for t in range(TILES):
        own_at = jnp.where(slot == t, order_ref[t], own_at)
        after = order_ref[t + 1] if t + 1 < TILES else jnp.int32(-1)
        before = order_ref[t - 1] if t > 0 else jnp.int32(-1)
        edge_at = jnp.where(slot == t, jnp.where(me < TILES // 2, after, before), edge_at)
    spot = iota((256, TILES * PIECE), 1)
    block = lax.shift_right_logical(spot * 205, 10)
    same = (spot - block * PIECE) == (iota((256, TILES * PIECE), 0) & 7)
    place[0] = jnp.where(same & (block == own_at), 1.0, 0.0).astype(BF16)
    place[1] = jnp.where(same & (block == edge_at), 1.0, 0.0).astype(BF16)

    for copies in halo:
        for copy in copies:
            copy.wait_send()
    for copy in (*x_copies, b_up, b_down):
        copy.wait_send()
    for k in range(1, TILES):
        block_copy(k).wait_send()

    for k in range(1, TILES):
        source = lax.rem(me + (TILES - k), TILES)
        pltpu.make_async_remote_copy(
            src_ref=tsend.at[source], dst_ref=trecv.at[source], send_sem=t_send.at[k],
            recv_sem=t_recv.at[k],
            device_id={"tile": source}, device_id_type=pl.DeviceIdType.MESH).wait_recv()
    got = trecv[...].astype(F32).reshape(TILES * 8, 128).T.astype(BF16)
    out_ref[...] = dot(got[:64], place[0]) + dot(got[64:], place[1])


def shards(latent, cached_latent, cached_features, reward_grad, conv_in_weight, conv_mid_weight,
           conv_up_weight, norm_gain, out_gain, shard_order):
    hbm = pl.BlockSpec(memory_space=pltpu.HBM)
    dma = pltpu.SemaphoreType.DMA
    call = pl.pallas_call(
        kernel,
        out_shape=pltpu.VMEM((4 * LAT, TILES * PIECE), F32),
        in_specs=[hbm] * 10,
        out_specs=pl.BlockSpec(memory_space=pltpu.VMEM),
        scratch_shapes=[
            pltpu.VMEM((3, ROWS + 4, LAT, COLS), BF16),
            pltpu.VMEM((3, ROWS + 2, COLS, MID), BF16),
            pltpu.VMEM((ROWS + 2, COLS, MID), BF16),
            pltpu.VMEM((ROWS + 2, COLS, MID), BF16),
            pltpu.VMEM((2 * ROWS + 2, OUT, 2 * COLS), BF16),
            pltpu.VMEM((2 * ROWS + 2, COLS, 2 * OUT), BF16),
            pltpu.VMEM((3, 3, 3, LAT, MID), BF16),
            pltpu.VMEM((3, 3, MID, 3 * MID), BF16),
            pltpu.VMEM((3, MID, 3 * MID), BF16),
            pltpu.VMEM((3, 3, OUT, MID), BF16),
            pltpu.VMEM((2, 4 * OUT, 2 * MID), BF16),
            pltpu.VMEM((1024, MID), BF16),
            pltpu.VMEM((ROWS + 2, COLS, MID), BF16),
            pltpu.VMEM((ROWS, 4, COLS + 16, 128), F32),
            pltpu.VMEM((TILES, 8, 128), BF16),
            pltpu.VMEM((TILES, 8, 128), BF16),
            pltpu.VMEM((2, 256, TILES * PIECE), BF16),
            pltpu.VMEM((2 * COLS, 3 * MID), F32),
            pltpu.VMEM((MID,), F32), pltpu.VMEM((OUT,), F32), pltpu.SMEM((TILES,), jnp.int32),
            dma((40,)), dma((2, 4)), dma((2, 4)), dma((2, 2)), dma((2, 2)),
            dma((2,)), dma((2,)), dma((TILES,)), dma((TILES,)),
            pltpu.SemaphoreType.REGULAR((4,)),
        ],
        compiler_params=pltpu.CompilerParams(
            collective_id=0, has_side_effects=True, vmem_limit_bytes=VMEM_LIMIT),
    )
    out = call(jnp.swapaxes(latent, 1, 2), jnp.swapaxes(cached_latent, 2, 3), cached_features,
               jnp.swapaxes(reward_grad, 1, 2), conv_in_weight, conv_mid_weight,
               jnp.swapaxes(conv_up_weight, 2, 3), norm_gain, out_gain, shard_order)
    return out.T


def solution(mesh):
    part = P(("prompt", "tile"), None, None)
    frames = P(None, ("prompt", "tile"), None, None)
    return jax.shard_map(
        shards,
        mesh=mesh,
        in_specs=(part, frames, frames, part, P(), P(), P(), P(), P(), P("prompt")),
        out_specs=P(("prompt", "tile"), None),
        check_vma=False,
    )
```

```python
import jax
import jax.numpy as jnp
from jax import lax
from jax.experimental import pallas as pl
from jax.experimental.pallas import tpu as pltpu
from jax.sharding import PartitionSpec as P

EPS = 1e-06
F32 = jnp.float32
BF16 = jnp.bfloat16
ROWS = 4
COLS = 160
LAT = 16
MID = 384
OUT = 192
TILES = 32
PIECE = 5
TOK = 80
CHUNKS = ((0, 256), (256, 128))
VMEM_LIMIT = 60 << 20


def hops(k):
    z = (k // 2) % 8
    return min(z, 8 - z) + (1 if 8 <= k < 24 else 0)


FAR_FIRST = sorted(range(1, TILES), key=lambda k: -hops(k))


def iota(shape, dim):
    return lax.broadcasted_iota(jnp.int32, shape, dim)


def down(x):
    return jnp.where(iota(x.shape, 0) == 0, 0.0, pltpu.roll(x, 1, 0))


def up(x):
    n = x.shape[0]
    return jnp.where(iota(x.shape, 0) == n - 1, 0.0, pltpu.roll(x, n - 1, 0))


def mixed(x, low, high):
    a, b, c = x[:, :128], x[:, 128:256], x[:, 256:]
    middle = jnp.where(iota(b.shape, 1) < 64, low(b), high(b))
    return jnp.concatenate([low(a), middle, high(c)], axis=1)


def halves_mean(x):
    a, b, c = x[:, :128], x[:, 128:256], x[:, 256:]
    left = iota(b.shape, 1) < 64
    first = jnp.sum(a + jnp.where(left, b, 0.0), axis=1, keepdims=True) * (1.0 / OUT)
    second = jnp.sum(c + jnp.where(left, 0.0, b), axis=1, keepdims=True) * (1.0 / OUT)
    return first, second


def spread(first, second, rows):
    left = iota((rows, 128), 1) < 64
    one = jnp.broadcast_to(first, (rows, 128))
    two = jnp.broadcast_to(second, (rows, 128))
    return jnp.concatenate([one, jnp.where(left, one, two), two], axis=1)


def cotangent(normed, half_gain, grad):
    q = normed * half_gain
    t = jnp.tanh(q)
    return (grad * half_gain) * ((1.0 + t) * (1.0 + q * (1.0 - t)))


def dot(a, b):
    return jnp.dot(a, b, preferred_element_type=F32)


def dot_t(a, b):
    return lax.dot_general(a, b, (((1,), (1,)), ((), ())), preferred_element_type=F32)


def kernel(
    lat_in, latc_in, feat_in, rew_in, win_in, wmid_in, wup_in, gain_in, ogain_in, order_in,
    out_ref,
    lat, feat, hid, xs, rew, rewp, win, wmid, wback, wup, fold, vt,
    bg, zs, tsend, trecv, place, acc, gain_ref, ogain_ref, order_ref,
    local_sem, halo_send, halo_recv, x_send, x_recv, b_send, b_recv,
    t_send, t_recv, know_sem,
):
    me = lax.axis_index("tile")

    def at(offset):
        return {"tile": lax.rem(me + (offset + TILES), TILES)}

    def signal(sem, offset):
        pl.semaphore_signal(sem, inc=1, device_id=at(offset), device_id_type=pl.DeviceIdType.MESH)

    def remote(src, dst, send, recv, offset):
        return pltpu.make_async_remote_copy(
            src_ref=src, dst_ref=dst, send_sem=send, recv_sem=recv,
            device_id=at(offset), device_id_type=pl.DeviceIdType.MESH,
        )

    local = []

    def load(src, dst):
        copy = pltpu.make_async_copy(src, dst, local_sem.at[len(local)])
        copy.start()
        local.append(copy)
        return copy

    barrier = pltpu.get_barrier_semaphore()
    signal(barrier, -1)
    signal(barrier, 1)
    load_lat = [
        load(lat_in, lat.at[2, pl.ds(2, ROWS)]),
        load(latc_in, lat.at[pl.ds(0, 2), pl.ds(2, ROWS)]),
    ]
    load_win = load(win_in, win)
    load_wup = load(wup_in, wup)
    load_rew = load(rew_in, rew.at[pl.ds(1, 2 * ROWS)])
    load_feat = load(feat_in, feat.at[pl.ds(0, 2), pl.ds(1, ROWS)])
    load_small = [load(gain_in, gain_ref), load(ogain_in, ogain_ref), load(order_in, order_ref)]
    load_mid = []
    for t in (0, 1, 2):
        for j in range(3):
            for start, width in CHUNKS:
                load_mid.append(load(
                    wmid_in.at[t, :, j, :, pl.ds(start, width)],
                    wmid.at[t, :, :, pl.ds(3 * start + j * width, width)]))
    pl.semaphore_wait(barrier, 2)
    halo = []
    for side, offset in ((0, -1), (1, 1)):
        row = 0 if side == 0 else ROWS - 2
        land = ROWS + 2 if side == 0 else 0
        copies = [
            remote(lat_in.at[pl.ds(row, 2)], lat.at[2, pl.ds(land, 2)],
                   halo_send.at[side, 0], halo_recv.at[side, 0], offset),
            remote(latc_in.at[:, pl.ds(row, 2)], lat.at[pl.ds(0, 2), pl.ds(land, 2)],
                   halo_send.at[side, 1], halo_recv.at[side, 1], offset),
        ]
        row = 0 if side == 0 else ROWS - 1
        land = ROWS + 1 if side == 0 else 0
        copies.append(
            remote(feat_in.at[:, pl.ds(row, 1)], feat.at[pl.ds(0, 2), pl.ds(land, 1)],
                   halo_send.at[side, 2], halo_recv.at[side, 2], offset))
        row = 0 if side == 0 else 2 * ROWS - 1
        land = 2 * ROWS + 1 if side == 0 else 0
        copies.append(
            remote(rew_in.at[pl.ds(row, 1)], rew.at[pl.ds(land, 1)],
                   halo_send.at[side, 3], halo_recv.at[side, 3], offset))
        halo.append(copies)
    for n in range(4):
        for side in range(2):
            halo[side][n].start()
    signal(know_sem.at[0], -1)
    signal(know_sem.at[0], 1)

    load_wup.wait()
    parts = []
    for i in range(3):
        k0, k1, k2 = (wup[i, j].astype(F32) for j in range(3))
        parts.append(jnp.concatenate([k0, k2, k1 + k2, k0 + k1], axis=0))
    fold[0, :, :MID] = parts[0].astype(BF16)
    fold[0, :, MID:] = (parts[1] + parts[2]).astype(BF16)
    fold[1, :, :MID] = (parts[0] + parts[1]).astype(BF16)
    fold[1, :, MID:] = parts[2].astype(BF16)

    load_rew.wait()
    n = iota((2 * COLS, 2 * COLS), 0)
    column = jnp.where(n < COLS, 2 * n, 2 * n - (2 * COLS - 1))
    parting = jnp.where(iota((2 * COLS, 2 * COLS), 1) == column, 1.0, 0.0).astype(BF16)
    left = iota((COLS, 128), 1) < 64

    def part_columns(ys):
        for y in ys:
            flat = jnp.concatenate([rew[y], jnp.zeros((256 - OUT, 2 * COLS), BF16)], axis=0)
            parted = dot_t(parting, flat)
            even, odd = parted[:COLS], parted[COLS:]
            o0, o1 = pltpu.roll(odd[:, :128], 64, 1), pltpu.roll(odd[:, 128:], 64, 1)
            rewp[y] = jnp.concatenate(
                [even[:, :128], jnp.where(left, even[:, 128:], o0), jnp.where(left, o0, o1)],
                axis=1).astype(BF16)

    part_columns(range(1, 2 * ROWS + 1))

    def frames(rows, times):
        return jnp.concatenate(
            [jnp.concatenate([feat[t, h + i] for t in times for i in range(3)], axis=1)
             for h in rows], axis=0)

    for copy in load_mid[:12] + [load_feat]:
        copy.wait()
    acc[...] = dot(frames((1, 2), (0, 1)), wmid[0:2].reshape(6 * MID, 3 * MID))

    for copy in load_lat + [load_win] + load_small:
        copy.wait()
    for n in range(2):
        for side in range(2):
            halo[side][n].wait_recv()

    @pl.when(me == 0)
    def _():
        lat[:, 0:2] = jnp.zeros((3, 2, LAT, COLS), BF16)

    @pl.when(me == TILES - 1)
    def _():
        lat[:, ROWS + 2:] = jnp.zeros((3, 2, LAT, COLS), BF16)

    taps = []
    for h in range(ROWS + 4):
        x = jnp.concatenate([lat[t, h].astype(F32) for t in range(3)], axis=0).T
        taps.append(jnp.concatenate([down(x), x, up(x)], axis=1).astype(BF16))
    total = None
    for i in range(3):
        weight = jnp.concatenate([win[t, i, j] for j in range(3) for t in range(3)], axis=0)
        part = dot(jnp.concatenate(taps[i:i + ROWS + 2], axis=0), weight)
        total = part if total is None else total + part
    half_gain = gain_ref[...].reshape(1, MID) * 0.5
    for h in range(ROWS + 2):
        value = total[h * COLS:(h + 1) * COLS].astype(BF16)
        hid[h] = value
        v = value.astype(F32)
        q = v * lax.rsqrt(jnp.mean(v * v, axis=1, keepdims=True) + EPS) * half_gain
        feat[2, h] = (q + q * jnp.tanh(q)).astype(BF16)

    for side in range(2):
        halo[side][2].wait_recv()

    @pl.when(me == 0)
    def _():
        feat[:, 0] = jnp.zeros((3, COLS, MID), BF16)

    @pl.when(me == TILES - 1)
    def _():
        feat[:, ROWS + 1] = jnp.zeros((3, COLS, MID), BF16)

    for copy in load_mid[12:]:
        copy.wait()
    load_back = []
    for i in range(3):
        load_back.append(load(wmid_in.at[2, i], wback.at[:, :, pl.ds(i * MID, MID)]))
    pl.semaphore_wait(know_sem.at[0], 2)
    signal(know_sem.at[1], -2)
    signal(know_sem.at[1], 2)

    def middle(rows, times, chunk, first=None):
        start, width = chunk
        depth = 3 * MID * len(times)
        lanes = slice(3 * start, 3 * (start + width))
        y = dot(frames(rows, times), wmid[times[0]:, :, :, lanes].reshape(depth, 3 * width))
        if first is not None:
            y = y + first[:, lanes]
        for n, h in enumerate(rows):
            z = y[n * COLS:(n + 1) * COLS]
            value = z[:, width:2 * width] + down(z[:, :width]) + up(z[:, 2 * width:])
            held = hid[h + 1, :, start:start + width].astype(F32)
            xs[h + 1, :, start:start + width] = (held + value).astype(BF16)

    x_copies = []
    for n, (start, width) in enumerate(CHUNKS):
        middle((0, 3), (0, 1, 2), (start, width))
        part = pl.ds(start, width)
        x_copies.append(remote(xs.at[1, :, part], xs.at[ROWS + 1, :, part],
                               x_send.at[n, 0], x_recv.at[n, 0], -1))
        x_copies.append(remote(xs.at[ROWS, :, part], xs.at[0, :, part],
                               x_send.at[n, 1], x_recv.at[n, 1], 1))
        x_copies[-2].start()
        x_copies[-1].start()
    for chunk in CHUNKS:
        middle((1, 2), (2,), chunk, acc)
    pl.semaphore_wait(know_sem.at[1], 2)
    signal(know_sem.at[2], -4)
    signal(know_sem.at[2], 4)
    half_ogain = ogain_ref[...].reshape(1, OUT) * 0.5
    half_ogain = jnp.concatenate([half_ogain, half_ogain], axis=1)

    def forward(a, rows):
        left = jnp.concatenate(
            [jnp.concatenate([xs[h + a], xs[h + a + 1]], axis=1) for h in rows], axis=0)
        return dot_t(left, fold[a])

    def pull(a, rows, y):
        lefts = []
        for n, h in enumerate(rows):
            z = y[n * COLS:(n + 1) * COLS]
            v = (z[:, MID:] + mixed(z[:, :MID], down, up)).astype(BF16).astype(F32)
            one, two = halves_mean(v * v)
            scale = spread(lax.rsqrt(one + EPS), lax.rsqrt(two + EPS), COLS)
            normed = v * scale
            t = cotangent(normed, half_ogain, rewp[2 * h + a + 1].astype(F32))
            one, two = halves_mean(t * normed)
            g = scale * (t - normed * spread(one, two, COLS))
            lefts.append(jnp.concatenate([mixed(g, up, down), g], axis=1).astype(BF16))
        return jnp.concatenate(lefts, axis=0)

    z0, z1 = zz = [{}, {}]

    def back(a, rows, left):
        z = dot(left, fold[a])
        for n, h in enumerate(rows):
            z_row = z[n * COLS:(n + 1) * COLS]
            zz[a][h] = (z_row[:, :MID], z_row[:, MID:])

    y0 = forward(0, (1, 3))
    y1 = forward(1, (0, 2))
    back(0, (1, 3), pull(0, (1, 3), y0))
    back(1, (0, 2), pull(1, (0, 2), y1))
    for side in range(2):
        halo[side][3].wait_recv()

    @pl.when(me == 0)
    def _():
        rew[0] = jnp.zeros((OUT, 2 * COLS), BF16)

    @pl.when(me == TILES - 1)
    def _():
        rew[2 * ROWS + 1] = jnp.zeros((OUT, 2 * COLS), BF16)

    part_columns((0, 2 * ROWS + 1))
    for copy in x_copies:
        copy.wait_recv()

    @pl.when(me == 0)
    def _():
        xs[0] = jnp.zeros((COLS, MID), BF16)

    @pl.when(me == TILES - 1)
    def _():
        xs[ROWS + 1] = jnp.zeros((COLS, MID), BF16)

    y1 = forward(1, (-1, 3))
    y0 = forward(0, (0, 4))
    left1 = pull(1, (-1, 3), y1)
    first = z0[1][0] + z1[0][0] + dot(left1[:COLS], fold[1, :, MID:])
    last = z0[3][1] + z1[2][1] + dot(left1[COLS:], fold[1, :, :MID])
    left0 = pull(0, (0, 4), y0)
    bg[1] = (first + dot(left0[:COLS], fold[0, :, MID:])).astype(BF16)
    bg[ROWS] = (last + dot(left0[COLS:], fold[0, :, :MID])).astype(BF16)
    b_up = remote(bg.at[1], bg.at[ROWS + 1], b_send.at[0], b_recv.at[0], -1)
    b_down = remote(bg.at[ROWS], bg.at[0], b_send.at[1], b_recv.at[1], 1)
    b_up.start()
    b_down.start()
    pl.semaphore_wait(know_sem.at[2], 2)
    signal(know_sem.at[3], -8)
    signal(know_sem.at[3], 8)
    y0 = forward(0, (2,))
    y1 = forward(1, (1,))
    back(0, (2,), pull(0, (2,), y0))
    back(1, (1,), pull(1, (1,), y1))
    for h in (1, 2):
        bg[h + 1] = (z0[h][1] + z0[h + 1][0] + z1[h][0] + z1[h - 1][1]).astype(BF16)

    r = iota((1024, 144), 0)
    par = lax.shift_right_logical(r, 9)
    d = lax.shift_right_logical(r, 7) & 3
    d = jnp.where(d == 3, -1, d)
    extra = lax.shift_right_logical(r, 6) & 1
    a = lax.shift_right_logical(r, 5) & 1
    b = lax.shift_right_logical(r, 4) & 1
    c = r & 15
    i = jnp.where(extra == 0, jnp.where(par == 0, a + 1, a), jnp.where(par == 0, 0, 2))
    fits = jnp.where(extra == 0, 1, jnp.where(par == 0, a, 1 - a))
    j = b - d + 1
    fits = jnp.where((j >= 0) & (j <= 2), fits, 0)
    want = jnp.where(fits == 1, i * 48 + j * 16 + c, -1)
    pick = jnp.where(iota((1024, 144), 1) == want, 1.0, 0.0).astype(BF16)
    vt[...] = dot(pick, win[2].reshape(144, MID)).astype(BF16)
    zs[:, :, 0:8] = jnp.zeros((ROWS, 4, 8, 128), F32)
    zs[:, :, COLS + 8:] = jnp.zeros((ROWS, 4, 8, 128), F32)

    for copy in load_back:
        copy.wait()

    def lower(rows):
        left = jnp.concatenate(
            [jnp.concatenate([bg[h + 2], bg[h + 1], bg[h]], axis=1) for h in rows], axis=0)
        y = dot_t(left, wback[...].reshape(3 * MID, 3 * MID))
        for n, h in enumerate(rows):
            z = y[n * COLS:(n + 1) * COLS]
            grad = z[:, MID:2 * MID] + up(z[:, :MID]) + down(z[:, 2 * MID:])
            v = hid[h + 1].astype(F32)
            scale = lax.rsqrt(jnp.mean(v * v, axis=1, keepdims=True) + EPS)
            normed = v * scale
            t = cotangent(normed, half_gain, grad)
            m = jnp.mean(t * normed, axis=1, keepdims=True)
            g = (bg[h + 1].astype(F32) + scale * (t - normed * m)).astype(BF16)
            last = dot_t(g, vt[(h % 2) * 512:(h % 2) * 512 + 512])
            for p in range(4):
                zs[h, p, 8:COLS + 8] = last[:, p * 128:(p + 1) * 128]

    lower((1, 2))
    b_up.wait_recv()
    b_down.wait_recv()

    @pl.when(me == 0)
    def _():
        bg[0] = jnp.zeros((COLS, MID), BF16)

    @pl.when(me == TILES - 1)
    def _():
        bg[ROWS + 1] = jnp.zeros((COLS, MID), BF16)

    lower((0, 3))

    def tokens(h):
        picks = ((0, 0), (1, 1), (2, 2), (3, -1))
        parts = [zs[h, n, pl.ds(8 + d, TOK, stride=2), :] for n, d in picks]
        return (parts[0] + parts[1]) + (parts[2] + parts[3])

    u0, u1, u2, u3 = (tokens(h) for h in range(ROWS))
    low = iota((TOK, 128), 1) < 64
    m0 = jnp.where(low, u0 + u1 + pltpu.roll(u2, 64, 1), u3)
    m1 = jnp.where(low, u2 + u3 + pltpu.roll(u1, 64, 1), u0)
    both = jnp.concatenate([m0, m1], axis=0).astype(BF16)
    row = iota((256, TILES * PIECE), 0)
    source = lax.shift_right_logical(row, 3) * PIECE + (row & 7)
    take = ((row & 7) < PIECE) & (iota((256, TILES * PIECE), 1) == source)
    blocks = dot(jnp.where(take, 1.0, 0.0).astype(BF16), both)
    tsend[...] = blocks.reshape(TILES, 8, 128).astype(BF16)

    pl.semaphore_wait(know_sem.at[3], 2)

    def block_copy(k):
        to = lax.rem(me + k, TILES)
        return pltpu.make_async_remote_copy(
            src_ref=tsend.at[to], dst_ref=trecv.at[me], send_sem=t_send.at[k],
            recv_sem=t_recv.at[k],
            device_id={"tile": to}, device_id_type=pl.DeviceIdType.MESH)

    for k in FAR_FIRST:
        block_copy(k).start()
    trecv[me] = tsend[me]

    slot = lax.shift_right_logical(iota((256, 1), 0), 3)
    own_at = jnp.full((256, 1), -1, jnp.int32)
    edge_at = jnp.full((256, 1), -1, jnp.int32)
    for t in range(TILES):
        own_at = jnp.where(slot == t, order_ref[t], own_at)
        after = order_ref[t + 1] if t + 1 < TILES else jnp.int32(-1)
        before = order_ref[t - 1] if t > 0 else jnp.int32(-1)
        edge_at = jnp.where(slot == t, jnp.where(me < TILES // 2, after, before), edge_at)
    spot = iota((256, TILES * PIECE), 1)
    block = lax.shift_right_logical(spot * 205, 10)
    same = (spot - block * PIECE) == (iota((256, TILES * PIECE), 0) & 7)
    place[0] = jnp.where(same & (block == own_at), 1.0, 0.0).astype(BF16)
    place[1] = jnp.where(same & (block == edge_at), 1.0, 0.0).astype(BF16)

    for copies in halo:
        for copy in copies:
            copy.wait_send()
    for copy in (*x_copies, b_up, b_down):
        copy.wait_send()
    for k in range(1, TILES):
        block_copy(k).wait_send()

    for k in range(1, TILES):
        source = lax.rem(me + (TILES - k), TILES)
        pltpu.make_async_remote_copy(
            src_ref=tsend.at[source], dst_ref=trecv.at[source], send_sem=t_send.at[k],
            recv_sem=t_recv.at[k],
            device_id={"tile": source}, device_id_type=pl.DeviceIdType.MESH).wait_recv()
    got = trecv[...].astype(F32).reshape(TILES * 8, 128).T.astype(BF16)
    out_ref[...] = dot(got[:64], place[0]) + dot(got[64:], place[1])


def shards(latent, cached_latent, cached_features, reward_grad, conv_in_weight, conv_mid_weight,
           conv_up_weight, norm_gain, out_gain, shard_order):
    hbm = pl.BlockSpec(memory_space=pltpu.HBM)
    dma = pltpu.SemaphoreType.DMA
    call = pl.pallas_call(
        kernel,
        out_shape=pltpu.VMEM((4 * LAT, TILES * PIECE), F32),
        in_specs=[hbm] * 10,
        out_specs=pl.BlockSpec(memory_space=pltpu.VMEM),
        scratch_shapes=[
            pltpu.VMEM((3, ROWS + 4, LAT, COLS), BF16),
            pltpu.VMEM((3, ROWS + 2, COLS, MID), BF16),
            pltpu.VMEM((ROWS + 2, COLS, MID), BF16),
            pltpu.VMEM((ROWS + 2, COLS, MID), BF16),
            pltpu.VMEM((2 * ROWS + 2, OUT, 2 * COLS), BF16),
            pltpu.VMEM((2 * ROWS + 2, COLS, 2 * OUT), BF16),
            pltpu.VMEM((3, 3, 3, LAT, MID), BF16),
            pltpu.VMEM((3, 3, MID, 3 * MID), BF16),
            pltpu.VMEM((3, MID, 3 * MID), BF16),
            pltpu.VMEM((3, 3, OUT, MID), BF16),
            pltpu.VMEM((2, 4 * OUT, 2 * MID), BF16),
            pltpu.VMEM((1024, MID), BF16),
            pltpu.VMEM((ROWS + 2, COLS, MID), BF16),
            pltpu.VMEM((ROWS, 4, COLS + 16, 128), F32),
            pltpu.VMEM((TILES, 8, 128), BF16),
            pltpu.VMEM((TILES, 8, 128), BF16),
            pltpu.VMEM((2, 256, TILES * PIECE), BF16),
            pltpu.VMEM((2 * COLS, 3 * MID), F32),
            pltpu.VMEM((MID,), F32), pltpu.VMEM((OUT,), F32), pltpu.SMEM((TILES,), jnp.int32),
            dma((40,)), dma((2, 4)), dma((2, 4)), dma((2, 2)), dma((2, 2)),
            dma((2,)), dma((2,)), dma((TILES,)), dma((TILES,)),
            pltpu.SemaphoreType.REGULAR((4,)),
        ],
        compiler_params=pltpu.CompilerParams(
            collective_id=0, has_side_effects=True, vmem_limit_bytes=VMEM_LIMIT),
    )
    out = call(jnp.swapaxes(latent, 1, 2), jnp.swapaxes(cached_latent, 2, 3), cached_features,
               jnp.swapaxes(reward_grad, 1, 2), conv_in_weight, conv_mid_weight,
               jnp.swapaxes(conv_up_weight, 2, 3), norm_gain, out_gain, shard_order)
    return out.T


def solution(mesh):
    part = P(("prompt", "tile"), None, None)
    frames = P(None, ("prompt", "tile"), None, None)
    return jax.shard_map(
        shards,
        mesh=mesh,
        in_specs=(part, frames, frames, part, P(), P(), P(), P(), P(), P("prompt")),
        out_specs=P(("prompt", "tile"), None),
        check_vma=False,
    )
```
